256 devices in a mesh: group: 64 (over x, z, core), batch: 4 (over y).
Axes of the slice: x: 4, y: 4, z: 8, core: 2. Of those that a mesh axis runs over, the one named last changes fastest.
Arguments:
- mixed_input: bfloat16 [65536, 2816], P(('batch', 'group')), parts along dimension 0, may hold values from -6 to 6
- conv_weight: float32 [4, 2816], replicated, may hold values from -3 to 3
- conv_bias: float32 [2816], replicated, may hold values from -3 to 3
- gate_input: bfloat16 [65536, 2560], P(('batch', 'group')), parts along dimension 0, may hold values from -6 to 6
- log_decay: float32 [40, 65536], P(None, ('batch', 'group')), parts along dimension 1, may hold values from -0.76 to 0, as said below
- level_weights: float32 [40, 20, 65536], P(None, None, ('batch', 'group')), parts along dimension 2, may hold values from 0.2 to 2
- skip_gain: float32 [40], replicated, may hold values from 0.3 to 3
- norm_gain: float32 [2560], replicated, may hold values from 0.25 to 1.75
- seg_lengths: int32 [12], P('batch'), parts along dimension 0, may hold values from 1 to 10240, 16384 in all
Outputs:
- output: bfloat16 [65536, 2560], P(('batch', 'group')), parts along dimension 0
The draws below stay inside these ranges and needn't reach their ends.
There are 4 independent parts, one for each index of `batch`. The reference program is written for one: setup_inputs(seed, part) draws one part's arguments, and reference() takes and returns one part's arrays. A program takes and returns all parts, laid end to end along the dimension named above; an argument that names none is the same for every part. Nothing has to cross between parts.
Inputs may be any that keep to these rules, and one draw needn't show every extreme that they name: `seg_lengths`: the recordings' lengths in order; they sum to 16384 and the longest is exactly 10240. `log_decay`: every entry is negative.
All inputs are finite; a program needn't handle non-finite values.
Results may differ from the reference program's by a relative error of at most 0.0034.
Values may be sent and summed in bfloat16 or wider, within the bound.
A program may use at most 128 MiB of HBM per device.

```python
import math
import jax
import jax.numpy as jnp
import numpy as np
from jax import lax

WIDTH = 2560
ATTENTION_UNITS = 40
HEAD_DIM = 64
STATE = 128
KERNEL = 4
LEVELS = 20
SEGS = 3
TOK_DEV = 256
RECORD_POSITIONS = 16384
CONV_CH = 2816
LONG = 10240


def draw_log_decay(key, part):
    addressing_vectors = jax.random.split(key, 6)
    fast_share = 0.5
    rough_lo = 0.5
    rough_hi = 1.5
    fast = jax.random.uniform(addressing_vectors[0], (ATTENTION_UNITS,), jnp.float32) < fast_share
    fast_rate = jnp.exp(jax.random.uniform(addressing_vectors[1], (ATTENTION_UNITS,), jnp.float32, jnp.log(1.0 / 50.0), jnp.log(1.0 / 30.0)))
    slow_rate = jnp.exp(jax.random.uniform(addressing_vectors[2], (ATTENTION_UNITS,), jnp.float32, jnp.log(0.03 / RECORD_POSITIONS), jnp.log(0.3 / RECORD_POSITIONS)))
    forgetting_speed = jnp.where(fast, fast_rate, slow_rate)
    rough_approximation = jax.random.uniform(addressing_vectors[3], (ATTENTION_UNITS, RECORD_POSITIONS), jnp.float32, rough_lo, rough_hi)
    echo_train = jax.random.uniform(addressing_vectors[4], (ATTENTION_UNITS, RECORD_POSITIONS), jnp.float32) < 4.0 / RECORD_POSITIONS
    fitting_objective = jnp.log(jax.random.uniform(addressing_vectors[5], (ATTENTION_UNITS, RECORD_POSITIONS), jnp.float32, 0.5, 0.8))
    return (-forgetting_speed[:, None] * rough_approximation + jnp.where(echo_train, fitting_objective, 0.0)).astype(jnp.float32)


def block_levels(key, extent, shards, least, high):
    level = 1.0
    for axis_at, blocks in shards:
        heights = jax.random.uniform(jax.random.fold_in(jax.random.fold_in(key, 6), axis_at), (blocks,), jnp.float32, least / len(shards), high / len(shards))
        level = level * jnp.repeat(jnp.exp(heights), extent[axis_at] // blocks).reshape((-1,) + (1,) * (len(extent) - 1 - axis_at))
    return level


def split_up(count, total, limit, slope):
    loads = [(1 << 20) // math.isqrt(grade ** slope) + 1 for grade in range(2, count + 1)]
    rest, given = total - limit - (count - 1), [1] * (count - 1)
    while rest > 0:
        movable = [i for i in range(count - 1) if given[i] < limit]
        pool, remaining = sum([loads[i] for i in movable]), rest
        for i in movable:
            addition = min(limit - given[i], max(1, remaining * loads[i] // pool), rest)
            given[i] = given[i] + addition
            rest = rest - addition
    return np.array([limit] + given)


def uneven(stream_key, number_of, total, bound, lean):
    if number_of == 2:
        one = jax.random.randint(stream_key, (), max(1, total - bound), min(bound, total - 1) + 1)
        return jnp.stack([one, total - one])
    sizes = jnp.asarray(split_up(number_of, total, bound, lean), jnp.int32)
    couples = (number_of - 1) // 2
    donor, receiver = sizes[1:1 + 2 * couples:2], sizes[2:2 + 2 * couples:2]
    margin = jnp.minimum(donor - 1, bound - receiver)
    passed = jax.random.randint(jax.random.fold_in(stream_key, 1), (couples,), 0, 1 << 20) % (margin + 1)
    sizes = sizes.at[1:1 + 2 * couples:2].set(donor - passed).at[2:2 + 2 * couples:2].set(receiver + passed)
    return sizes[jax.random.permutation(jax.random.fold_in(stream_key, 2), number_of)]


def bell_draw(key, extent, width, limit, cuts=(), kind=jnp.bfloat16):
    values = width * jax.random.normal(key, extent, jnp.float32)
    if cuts:
        values = values * block_levels(key, extent, cuts, -0.22, 0.18)
    return jnp.clip(values, -limit, limit).astype(kind)


def setup_inputs(seed: int = 0, part: int = 0) -> dict:
    key_of = jax.random.split(jax.random.key(seed), 10)
    own_keys = jax.random.split(jax.random.fold_in(key_of[9], part), 10)
    mixed_input = bell_draw(own_keys[0], (RECORD_POSITIONS, CONV_CH), 1.0, 6.0, ((0, 64),))
    conv_weight = bell_draw(key_of[1], (KERNEL, CONV_CH), KERNEL ** -0.5, 3.0, (), jnp.float32)
    conv_bias = bell_draw(key_of[2], (CONV_CH,), 0.5, 3.0, (), jnp.float32)
    gate_input = bell_draw(own_keys[3], (RECORD_POSITIONS, WIDTH), 1.0, 6.0, ((0, 64),))
    log_decay = draw_log_decay(jax.random.fold_in(jax.random.fold_in(key_of[9], part), 71), part)
    level_weights = jnp.clip(jnp.exp(math.log(2.0) - 2.3025851 * jax.random.uniform(own_keys[5], (ATTENTION_UNITS, LEVELS, RECORD_POSITIONS), jnp.float32) ** block_levels(own_keys[5], (ATTENTION_UNITS, LEVELS, RECORD_POSITIONS), ((2, 64),), -0.2, 0.2)), 0.2, 2.0)
    skip_gain = jnp.clip(jnp.exp(jax.random.uniform(key_of[6], (ATTENTION_UNITS,), jnp.float32, math.log(0.3), math.log(3.0))), 0.3, 3.0)
    norm_gain = jnp.clip(1.0 + 0.15 * jax.random.normal(key_of[7], (WIDTH,), jnp.float32), 0.25, 1.75)
    seg_lengths = uneven(own_keys[8], SEGS, RECORD_POSITIONS, LONG, 0).astype(jnp.int32)
    return {"mixed_input": mixed_input, "conv_weight": conv_weight, "conv_bias": conv_bias, "gate_input": gate_input, "log_decay": log_decay, "level_weights": level_weights, "skip_gain": skip_gain, "norm_gain": norm_gain, "seg_lengths": seg_lengths}


def segment_of(positions, seg_lengths):
    bounds = jnp.cumsum(seg_lengths)[:-1].astype(jnp.int32)
    found = lax.optimization_barrier(jnp.sum((positions[:, None] >= bounds[None, :]).astype(jnp.int32), axis=1)).astype(jnp.int32)
    return jnp.where(positions >= 0, found, -1).astype(jnp.int32)

def pair_levels(count, low_bits):
    index = jnp.arange(count, dtype=jnp.int32)
    diff = jnp.bitwise_xor(index[:, None], index[None, :])
    levels = jnp.zeros((count, count), jnp.int32)
    for bit_index in range(low_bits):
        levels = levels + (diff >= 2 ** bit_index).astype(jnp.int32)
    return levels

def convolve(rows, segs, conv_weight, conv_bias, taps):
    count = rows.shape[0] - (taps - 1)
    total = jnp.zeros((count, rows.shape[1]), jnp.float32) + conv_bias[None, :]
    for tap in range(taps):
        begin = taps - 1 - tap
        piece = rows[begin:begin + count].astype(jnp.float32)
        same = (segs[begin:begin + count] == segs[taps - 1:]).astype(jnp.float32)
        total = total + conv_weight[tap][None, :] * piece * same[:, None]
    return jax.nn.silu(total)

def reference(mixed_input, conv_weight, conv_bias, gate_input, log_decay, level_weights, skip_gain, norm_gain, seg_lengths):
    tok_rows = TOK_DEV
    group_count = RECORD_POSITIONS // tok_rows
    low_bits = tok_rows.bit_length() - 1
    high_bits = group_count.bit_length() - 1
    head_count = ATTENTION_UNITS
    head_dim = HEAD_DIM
    positions = jnp.arange(RECORD_POSITIONS, dtype=jnp.int32)
    segs = segment_of(positions, seg_lengths)
    padded_rows = jnp.concatenate([jnp.zeros((KERNEL - 1, CONV_CH), mixed_input.dtype), mixed_input], axis=0)
    padded_segs = jnp.concatenate([jnp.full((KERNEL - 1,), -1, jnp.int32), segs], axis=0)
    activated = convolve(padded_rows, padded_segs, conv_weight, conv_bias, KERNEL)
    xs = activated[:, :WIDTH].astype(jnp.bfloat16)
    keys = activated[:, WIDTH:WIDTH + STATE].astype(jnp.bfloat16)
    queries = activated[:, WIDTH + STATE:].astype(jnp.bfloat16)
    cum = jnp.cumsum(log_decay.reshape(head_count, group_count, tok_rows), axis=2)
    seg_groups = segs.reshape(group_count, tok_rows)
    last_seg = seg_groups[:, -1]
    prev_seg = jnp.concatenate([jnp.full((1,), -1, jnp.int32), last_seg[:-1]])
    through = jnp.exp(cum[:, :, -1]).T * (last_seg == prev_seg).astype(jnp.float32)[:, None]
    x_groups = xs.reshape(group_count, tok_rows, head_count, head_dim)
    k_groups = keys.reshape(group_count, tok_rows, STATE)
    q_groups = queries.reshape(group_count, tok_rows, STATE)
    cum_groups = jnp.transpose(cum, (1, 0, 2))
    lam_groups = jnp.transpose(level_weights.reshape(head_count, LEVELS, group_count, tok_rows), (2, 0, 1, 3))
    gate_groups = gate_input.reshape(group_count, tok_rows, WIDTH)

    def end_state(items):
        x_part, k_part, cum_part, seg_part = items
        same = (seg_part == seg_part[-1]).astype(jnp.float32)
        weight = jnp.exp(cum_part[:, -1:] - cum_part) * same[None, :]
        scaled = (x_part.astype(jnp.float32) * weight.T[:, :, None]).astype(jnp.bfloat16)
        return jnp.einsum('sn,shp->hnp', k_part.astype(jnp.float32), scaled.astype(jnp.float32))
    states = lax.map(end_state, (x_groups, k_groups, cum_groups, seg_groups))
    pair_level = pair_levels(tok_rows, low_bits)
    row_ids = jnp.arange(tok_rows, dtype=jnp.int32)
    lower_tri = row_ids[None, :] <= row_ids[:, None]
    group_ids = jnp.arange(group_count, dtype=jnp.int32)

    def one_group(items):
        index, x_part, k_part, q_part, cum_part, seg_part, lam_part, gate_part, prev_part = items
        scores = jnp.dot(q_part, k_part.T, preferred_element_type=jnp.float32)
        valid = lower_tri & (seg_part[:, None] == seg_part[None, :])
        gap = jnp.where(valid[None], cum_part[:, :, None] - cum_part[:, None, :], 0.0)
        decay = jnp.exp(gap) * valid[None].astype(jnp.float32)
        picked = jnp.transpose(lam_part, (0, 2, 1))[:, row_ids[:, None], pair_level]
        mixing = lax.optimization_barrier((scores[None] * picked * decay).astype(jnp.bfloat16))
        result = jnp.einsum('hts,shp->thp', mixing.astype(jnp.float32), x_part.astype(jnp.float32))
        alive = (seg_part == prev_part).astype(jnp.float32)
        entry = jnp.exp(cum_part) * alive[None, :]
        open_through = jnp.where((group_ids < index)[:, None], through, 1.0)
        carried = jnp.cumprod(open_through[::-1], axis=0)[::-1]
        suffix = jnp.concatenate([carried[1:], jnp.ones((1, head_count), jnp.float32)], axis=0)
        for bit_index in range(high_bits):
            size = 2 ** bit_index
            is_set = index // size % 2 == 1
            first = index // (2 * size) * (2 * size)
            inside = (group_ids >= first) & (group_ids < first + size) & is_set
            weights = jnp.where(inside[:, None], suffix, 0.0)
            level_state = jnp.einsum('jh,jhnp->hnp', weights, states, precision=lax.Precision.HIGHEST)
            level_half = lax.optimization_barrier(level_state.astype(jnp.bfloat16))
            read = jnp.einsum('tn,hnp->thp', q_part.astype(jnp.float32), level_half.astype(jnp.float32))
            coef = lam_part[:, low_bits + 1 + bit_index, :] * entry
            result = result + read * coef.T[:, :, None]
        result = result + skip_gain[None, :, None] * x_part.astype(jnp.float32)
        flat = result.reshape(tok_rows, WIDTH)
        gated = flat * jax.nn.silu(gate_part.astype(jnp.float32))
        scale = lax.rsqrt(lax.optimization_barrier(jnp.mean(gated * gated, axis=1, keepdims=True)) + 1e-05)
        return (gated * scale * norm_gain[None, :]).astype(jnp.bfloat16)
    output = lax.map(one_group, (group_ids, x_groups, k_groups, q_groups, cum_groups, seg_groups, lam_groups, gate_groups, prev_seg))
    return output.reshape(RECORD_POSITIONS, WIDTH)
```

```python
import jax
import jax.numpy as jnp
from jax import lax
from jax.experimental import pallas as pl
from jax.experimental.pallas import tpu as pltpu
from jax.sharding import PartitionSpec as P

EPS = 1e-05
F32 = jnp.float32
BF16 = jnp.bfloat16
MESH = pl.DeviceIdType.MESH

TOK = 256
WIDTH = 2560
HEADS = 40
HD = 64
STATE = 128
CH = 2816
TAPS = 4
NX, NZ = 4, 8
HALF = WIDTH // 2
HALO = 16
CR = 128
NC = HALF // CR
HPC = CR // HD
XR = CR + 16
BR = 256
NB = WIDTH // BR
HPB = BR // HD

L1, L2, L3, TT, X4, X5 = range(6)


def kernel(
    mixed,
    gate,
    ld,
    lam,
    cw,
    cb,
    ng,
    skip,
    segl,
    out,
    halo,
    pad,
    xst,
    keys,
    quer,
    ef,
    sibe,
    cacc,
    snd,
    lbuf,
    tbuf,
    dec,
    dsrc,
    theta,
    pbuf,
    cum,
    cumt,
    endw,
    entry,
    sct,
    lev,
    acc,
    gt,
    halo_s,
    halo_r,
    th_s,
    th_r,
    e_s,
    e_r,
    rsem,
    ssem,
    ssem2,
    sib_s,
    sib_r,
):
    g = lax.axis_index("group")
    core = lax.rem(g, 2)
    z = lax.rem(g // 2, NZ)
    x = g // (2 * NZ)
    ngroups = 2 * NZ * NX

    def at(xx, zz, cc):
        return (xx * NZ + zz) * 2 + cc

    sib = at(x, z, 1 - core)
    zup = at(x, lax.rem(z + 1, NZ), core)
    zdn = at(x, lax.rem(z + NZ - 1, NZ), core)
    zup3 = at(x, lax.rem(z + 3, NZ), core)
    zdn3 = at(x, lax.rem(z + NZ - 3, NZ), core)
    xup = at(lax.rem(x + 1, NX), z, core)
    xdn = at(lax.rem(x + NX - 1, NX), z, core)
    gnext = lax.rem(g + 1, ngroups)
    gprev = lax.rem(g + ngroups - 1, ngroups)

    barrier = pltpu.get_barrier_semaphore()
    partners = (sib, zup, zdn, zup3, zdn3, xup, xdn, gnext, gprev)
    for peer in partners:
        pl.semaphore_signal(barrier, inc=1, device_id={"group": peer}, device_id_type=MESH)

    def rcopy(src, dst, ss, rs, peer):
        return pltpu.make_async_remote_copy(
            src_ref=src,
            dst_ref=dst,
            send_sem=ss,
            recv_sem=rs,
            device_id={"group": peer},
            device_id_type=MESH,
        )

    first = g * TOK
    b1 = segl[0]
    b2 = segl[0] + segl[1]

    def seg_of(pos):
        s = (pos >= b1).astype(jnp.int32) + (pos >= b2).astype(jnp.int32)
        return jnp.where(pos >= 0, s, -1)

    lane_pos = first + lax.broadcasted_iota(jnp.int32, (8, TOK), 1)[0:1]
    seg_row = seg_of(lane_pos)
    last_row = seg_of(jnp.full((1, TOK), first + TOK - 1, jnp.int32))
    prev_row = seg_of(jnp.full((1, TOK), first - 1, jnp.int32))

    c = ld[...]
    lane = lax.broadcasted_iota(jnp.int32, (HEADS, TOK), 1)
    step = 1
    while step < TOK:
        c = c + jnp.where(lane >= step, pltpu.roll(c, step, 1), 0.0)
        step *= 2
    cum[...] = c
    c_end = c[:, TOK - 1 : TOK]
    endw[...] = jnp.exp(c_end - c) * (seg_row == last_row).astype(F32)
    entry[...] = jnp.exp(c) * (seg_row == prev_row).astype(F32)
    theta[0] = jnp.broadcast_to(jnp.exp(c_end), (HEADS, 128)) * (last_row == prev_row).astype(F32)[
        :, 0:128
    ]
    cpad = jnp.concatenate([c, jnp.zeros((128 - HEADS, TOK), F32)], axis=0)
    cumt[...] = jnp.concatenate([cpad[:, 0:128].T, cpad[:, 128:256].T], axis=0)

    si = lax.broadcasted_iota(jnp.int32, (128, 128), 0)
    ti = lax.broadcasted_iota(jnp.int32, (128, 128), 1)
    diff = si ^ ti
    lv = jnp.zeros((128, 128), jnp.int32)
    for b in range(7):
        lv = lv + (diff >= 2**b).astype(jnp.int32)
    lev[...] = lv

    pl.semaphore_wait(barrier, len(partners))

    halo_copy = rcopy(mixed.at[pl.ds(TOK - HALO, HALO)], halo, halo_s, halo_r, gnext)
    halo_copy.start()
    th_copy = rcopy(theta.at[0], theta.at[1], th_s, th_r, sib)
    th_copy.start()

    col_pos = first + lax.broadcasted_iota(jnp.int32, (TOK, 256), 0)
    seg_col = seg_of(col_pos)
    same = [None] + [seg_of(col_pos - t) == seg_col for t in range(1, TAPS)]

    def conv(cols):
        cur = mixed[:, cols].astype(F32)
        pad[8 : 8 + TOK, :] = cur
        pad[0:8, :] = halo[HALO - 8 : HALO, cols].astype(F32)
        total = cb[:, cols] + cw[0:1, cols] * cur
        for t in range(1, TAPS):
            piece = pad[8 - t : 8 - t + TOK, :]
            total = total + cw[t : t + 1, cols] * jnp.where(same[t], piece, 0.0)
        return total * (1.0 / (1.0 + jnp.exp(-total)))

    halo_copy.wait_recv()
    kq = conv(pl.ds(WIDTH, 2 * STATE))
    keys[...] = kq[:, 0:STATE].astype(BF16)
    quer[...] = kq[:, STATE : 2 * STATE].astype(BF16)

    def e_copy(i):
        rows = pl.ds(pl.multiple_of(i * BR, BR), BR)
        return rcopy(ef.at[rows], sibe.at[rows], e_s.at[i], e_r.at[i], sib)

    def conv_step(i, _):
        base = pl.multiple_of(i * BR, BR)
        act = conv(pl.ds(base, BR)).T.astype(BF16)
        xst[pl.ds(base, BR), :] = act
        parts = []
        for j in range(HPB):
            w = endw[pl.ds(i * HPB + j, 1), :]
            parts.append((act[j * HD : (j + 1) * HD].astype(F32) * w).astype(BF16))
        e = jnp.dot(jnp.concatenate(parts, axis=0), keys[...], preferred_element_type=F32)
        ef[pl.ds(base, BR), :] = e
        e_copy(i).start()
        return 0

    lax.fori_loop(0, NB, conv_step, 0)

    th_copy.wait_recv()
    dsrc[0] = theta[0] * theta[1]
    pbuf[0] = jnp.ones((HEADS, 128), F32)

    @pl.when(core == 1)
    def _():
        pbuf[1] = theta[1]

    @pl.when(core == 0)
    def _():
        pbuf[1] = jnp.ones((HEADS, 128), F32)

    half = core * HALF

    def mine(i):
        return pl.ds(pl.multiple_of(half + i * CR, CR), CR)

    def sub(i):
        return pl.ds(pl.multiple_of(i * CR, CR), CR)

    def chunk(i):
        return core * NC + i

    def lcopy(s, i, peer, ss):
        dst = lbuf.at[s, chunk(i)]
        return rcopy(dst, dst, ss.at[s, i], rsem.at[s, i], peer)

    def scopy(k, s, i, peer, ss):
        return rcopy(snd.at[k, i], lbuf.at[s, chunk(i)], ss.at[s, i], rsem.at[s, i], peer)

    def dcopy(src, slot, s, peer, ss):
        return rcopy(src, dec.at[slot], ss.at[s, NC], rsem.at[s, NC], peer)

    def sibcopy(k, s, i):
        dst = lbuf.at[k, chunk(i)]
        return rcopy(dst, dst, sib_s.at[s, i], sib_r.at[s, i], sib)

    def sibwait(k, s, i):
        dst = lbuf.at[k, (1 - core) * NC + i]
        rcopy(dst, dst, sib_s.at[s, i], sib_r.at[s, i], sib).wait_recv()

    def tcopy(i, peer, ss):
        dst = tbuf.at[i]
        return rcopy(dst, dst, ss.at[TT, i], rsem.at[TT, i], peer)

    def x4copy(i):
        return rcopy(
            tbuf.at[i], lbuf.at[3, chunk(i)], ssem.at[X4, i], rsem.at[X4, i], xup
        )

    def encode(v):
        q, ex = [], []
        for j in range(HPC):
            blk = v[j * HD : (j + 1) * HD]
            top = jnp.max(jnp.abs(blk), axis=0, keepdims=True)
            e = jnp.ceil(jnp.log2(jnp.maximum(top, 1e-30))) - 14.0
            q.append(jnp.floor(blk * (1.0 / jnp.exp2(e)) + 0.5))
            ex.append(jnp.broadcast_to(e, (16 // HPC, 128)))
        return jnp.concatenate(q + ex, axis=0).astype(jnp.int32).astype(jnp.int16)

    def decode(ref):
        v = ref[...].astype(jnp.int32).astype(F32)
        parts = []
        for j in range(HPC):
            r = CR + j * (16 // HPC)
            parts.append(v[j * HD : (j + 1) * HD] * jnp.exp2(v[r : r + 1]))
        return jnp.concatenate(parts, axis=0)

    def scaled_add(recv, dref, base, i):
        rows = []
        for j in range(HPC):
            h = core * (HEADS // 2) + i * HPC + j
            d = dref[pl.ds(h, 1), :]
            rows.append(recv[j * HD : (j + 1) * HD] * d + base[j * HD : (j + 1) * HD])
        return jnp.concatenate(rows, axis=0)

    is_even = lax.rem(z, 2) == 0
    z4 = lax.rem(z, 4)

    @pl.when(is_even)
    def _():
        dcopy(dsrc.at[0], 0, L1, zup, ssem).start()

    def wait_e(i, _):
        e_copy(i).wait_recv()
        return 0

    lax.fori_loop(0, NB, wait_e, 0)

    def chip_step(i, _):
        rows = mine(i)
        own = ef[rows, :]
        other = sibe[rows, :]

        @pl.when(core == 1)
        def _():
            cacc[sub(i), :] = scaled_add(other, theta.at[0], own, i)

        @pl.when(core == 0)
        def _():
            cacc[sub(i), :] = scaled_add(own, theta.at[1], other, i)

        @pl.when(is_even)
        def _():
            snd[0, i] = encode(cacc[sub(i), :])
            scopy(0, 0, i, zup, ssem).start()

        return 0

    lax.fori_loop(0, NC, chip_step, 0)

    s_t = lax.dot_general(
        keys[...], quer[...], (((1,), (1,)), ((), ())), preferred_element_type=F32
    )
    rowi = lax.broadcasted_iota(jnp.int32, (TOK, TOK), 0)
    coli = lax.broadcasted_iota(jnp.int32, (TOK, TOK), 1)
    ok = (rowi <= coli) & (seg_col == seg_row)
    sct[...] = jnp.where(ok, s_t, 0.0)

    def local_heads(i):
        rolled = pltpu.roll(cumt[...], lax.rem(128 - i * HPB, 128), 1)
        for j in range(HPB):
            h = i * HPB + j
            rows = pl.ds(pl.multiple_of(h * HD, HD), HD)
            ccol = rolled[:, j : j + 1]
            crow = cum[pl.ds(h, 1), :]

            def lam_row(l, lo):
                return lam[h, l : l + 1, lo : lo + 128]

            def picked(lo):
                p = jnp.broadcast_to(lam_row(7, lo), (128, 128))
                for l in range(7):
                    p = jnp.where(lev[...] == l, lam_row(l, lo), p)
                return p

            def mix(slo, tlo, pick):
                gap = crow[:, tlo : tlo + 128] - ccol[slo : slo + 128]
                decay = jnp.exp(jnp.minimum(gap, 0.0))
                return (sct[slo : slo + 128, tlo : tlo + 128] * pick * decay).astype(BF16)

            m00 = mix(0, 0, picked(0))
            m01 = mix(0, 128, lam_row(8, 128))
            m11 = mix(128, 128, picked(128))
            xs = xst[rows, :]
            left = jnp.dot(xs[:, 0:128], m00, preferred_element_type=F32)
            right = jnp.dot(xs, jnp.concatenate([m01, m11], axis=0), preferred_element_type=F32)
            acc[rows, :] = jnp.concatenate([left, right], axis=1) + skip[h] * xs.astype(F32)

    @pl.when(is_even)
    def _():
        pbuf[2] = pbuf[1]

    @pl.when(jnp.logical_not(is_even))
    def _():
        dcopy(dsrc.at[0], 0, L1, zup, ssem).wait_recv()
        pbuf[2] = pbuf[1] * dec[0]
        dsrc[1] = dec[0] * dsrc[0]

        @pl.when(z4 == 1)
        def _():
            dcopy(dsrc.at[1], 1, L2, zup, ssem).start()

    def l1_step(i, _):
        local_heads(i)

        @pl.when(jnp.logical_not(is_even))
        def _():
            scopy(0, 0, i, zup, ssem).wait_recv()
            sibcopy(0, L1, i).start()
            s = scaled_add(decode(lbuf.at[0, chunk(i)]), dsrc.at[0], cacc[sub(i), :], i)
            cacc[sub(i), :] = s

            @pl.when(z4 == 1)
            def _():
                snd[1, i] = encode(s)
                scopy(1, 1, i, zup, ssem).start()

        return 0

    lax.fori_loop(0, NC, l1_step, 0)

    @pl.when(z4 < 2)
    def _():
        pbuf[3] = pbuf[2]

    @pl.when(z4 >= 2)
    def _():
        dcopy(dec.at[1], 1, L2, zup, ssem).wait_recv()
        pbuf[3] = pbuf[2] * dec[1]

        @pl.when(z4 == 2)
        def _():
            dcopy(dec.at[1], 1, L2, zup, ssem).start()

        @pl.when(z4 == 3)
        def _():
            dsrc[2] = dec[1] * dsrc[1]

            @pl.when(z == 3)
            def _():
                dcopy(dsrc.at[2], 2, L3, zup, ssem).start()
                dcopy(dsrc.at[2], 2, L3, zdn3, ssem2).start()

    def gate_block(i):
        cols = pl.ds(pl.multiple_of(i * BR, BR), BR)
        v = gate[:, cols].astype(F32)
        gt[cols, :] = (v * (1.0 / (1.0 + jnp.exp(-v)))).T

    def l2_step(i, _):
        gate_block(i)

        @pl.when(z4 >= 2)
        def _():
            lcopy(1, i, zup, ssem).wait_recv()

            @pl.when(z4 == 2)
            def _():
                lcopy(1, i, zup, ssem).start()

            sibcopy(1, L2, i).start()

            @pl.when(z4 == 3)
            def _():
                s = scaled_add(decode(lbuf.at[1, chunk(i)]), dsrc.at[1], cacc[sub(i), :], i)
                cacc[sub(i), :] = s

                @pl.when(z == 3)
                def _():
                    snd[2, i] = encode(s)
                    scopy(2, 2, i, zup, ssem).start()
                    scopy(2, 2, i, zdn3, ssem2).start()

        return 0

    lax.fori_loop(0, NC, l2_step, 0)

    l3_in = jnp.logical_or(z >= 4, z == 0)

    def l3_relay(make):
        @pl.when(z == 4)
        def _():
            make(zup)

        @pl.when(jnp.logical_or(z == 0, z == 7))
        def _():
            make(zdn)

    @pl.when(z < 4)
    def _():
        pbuf[4] = pbuf[3]

    @pl.when(l3_in)
    def _():
        dcopy(dec.at[2], 2, L3, zup, ssem).wait_recv()
        l3_relay(lambda peer: dcopy(dec.at[2], 2, L3, peer, ssem).start())

        @pl.when(z >= 4)
        def _():
            pbuf[4] = pbuf[3] * dec[2]

        @pl.when(z == 7)
        def _():
            dec[3] = dec[2] * dsrc[2]

            @pl.when(x < NX - 1)
            def _():
                dcopy(dec.at[3], 3, TT, zup, ssem).start()
                dcopy(dec.at[3], 3, TT, zdn, ssem2).start()

                @pl.when(lax.rem(x, 2) == 0)
                def _():
                    dcopy(dec.at[3], 4, X4, xup, ssem).start()

    def l3_step(i, _):
        @pl.when(l3_in)
        def _():
            lcopy(2, i, zup, ssem).wait_recv()
            l3_relay(lambda peer: lcopy(2, i, peer, ssem).start())

            @pl.when(z >= 4)
            def _():
                sibcopy(2, L3, i).start()

            @pl.when(z == 7)
            def _():
                s = scaled_add(decode(lbuf.at[2, chunk(i)]), dsrc.at[2], cacc[sub(i), :], i)
                tbuf[i] = encode(s)

                @pl.when(x < NX - 1)
                def _():
                    tcopy(i, zup, ssem).start()
                    tcopy(i, zdn, ssem2).start()

                    @pl.when(lax.rem(x, 2) == 0)
                    def _():
                        x4copy(i).start()

        return 0

    lax.fori_loop(0, NC, l3_step, 0)

    t_in = jnp.logical_and(z < 7, x < NX - 1)

    def t_relay(make):
        @pl.when(z <= 2)
        def _():
            make(zup)

        @pl.when(z >= 5)
        def _():
            make(zdn)

    @pl.when(t_in)
    def _():
        dcopy(dec.at[3], 3, TT, zup, ssem).wait_recv()
        t_relay(lambda peer: dcopy(dec.at[3], 3, TT, peer, ssem).start())

        @pl.when(lax.rem(x, 2) == 0)
        def _():
            dcopy(dec.at[3], 4, X4, xup, ssem).start()

    def t_step(i, _):
        @pl.when(t_in)
        def _():
            tcopy(i, zup, ssem).wait_recv()
            t_relay(lambda peer: tcopy(i, peer, ssem).start())

            @pl.when(lax.rem(x, 2) == 0)
            def _():
                x4copy(i).start()

        return 0

    lax.fori_loop(0, NC, t_step, 0)

    def far(level):
        def body(i, _):
            base = pl.multiple_of(i * BR, BR)
            if level == 0:
                state = sibe[pl.ds(base, BR), :].astype(BF16)
            else:
                parts = []
                for m in range(HPB // HPC):
                    v = decode(lbuf.at[level - 1, i * (HPB // HPC) + m])
                    for j in range(HPC):
                        p = pbuf[level, pl.ds(i * HPB + m * HPC + j, 1), :]
                        parts.append((v[j * HD : (j + 1) * HD] * p).astype(BF16))
                state = jnp.concatenate(parts, axis=0)
            read = lax.dot_general(
                state, quer[...], (((1,), (1,)), ((), ())), preferred_element_type=F32
            )
            for j in range(HPB):
                h = i * HPB + j
                coef = lam[h, 9 + level : 10 + level, :] * entry[pl.ds(h, 1), :]
                rows = pl.ds(pl.multiple_of(base + j * HD, HD), HD)
                acc[rows, :] = acc[rows, :] + read[j * HD : (j + 1) * HD] * coef
            return 0

        lax.fori_loop(0, NB, body, 0)

    def sib_wait_all(k, s):
        def body(i, _):
            sibwait(k, s, i)
            return 0

        lax.fori_loop(0, NC, body, 0)

    @pl.when(core == 1)
    def _():
        far(0)

    @pl.when(jnp.logical_not(is_even))
    def _():
        sib_wait_all(0, L1)
        far(1)

    @pl.when(z4 >= 2)
    def _():
        sib_wait_all(1, L2)
        far(2)

    @pl.when(z >= 4)
    def _():
        sib_wait_all(2, L3)
        far(3)

    x_odd = lax.rem(x, 2) == 1

    @pl.when(jnp.logical_not(x_odd))
    def _():
        pbuf[5] = pbuf[4]

    @pl.when(x_odd)
    def _():
        dcopy(dec.at[3], 4, X4, xup, ssem).wait_recv()
        pbuf[5] = pbuf[4] * dec[4]

    def x5copy(i, peer, ss):
        return rcopy(snd.at[3, i], lbuf.at[4, chunk(i)], ss.at[X5, i], rsem.at[X5, i], peer)

    def x5relay(i):
        dst = lbuf.at[4, chunk(i)]
        return rcopy(dst, dst, ssem.at[X5, i], rsem.at[X5, i], xdn)

    def x4_step(i, _):
        @pl.when(x_odd)
        def _():
            x4copy(i).wait_recv()
            sibcopy(3, X4, i).start()

            @pl.when(x == 1)
            def _():
                s = scaled_add(
                    decode(lbuf.at[3, chunk(i)]), dec.at[3], decode(tbuf.at[i]), i
                )
                snd[3, i] = encode(s)
                x5copy(i, xup, ssem).start()
                x5copy(i, xdn, ssem2).start()

        return 0

    lax.fori_loop(0, NC, x4_step, 0)

    def x5_step(i, _):
        @pl.when(x != 1)
        def _():
            x5relay(i).wait_recv()

            @pl.when(x == 0)
            def _():
                x5relay(i).start()

            @pl.when(x >= 2)
            def _():
                sibcopy(4, X5, i).start()

        return 0

    @pl.when(x_odd)
    def _():
        sib_wait_all(3, X4)
        far(4)

    lax.fori_loop(0, NC, x5_step, 0)

    @pl.when(x >= 2)
    def _():
        sib_wait_all(4, X5)
        far(5)

    def gate_step(i, ssq):
        rows = pl.ds(pl.multiple_of(i * BR, BR), BR)
        v = acc[rows, :] * gt[rows, :]
        acc[rows, :] = v
        return ssq + jnp.sum((v * v).reshape(BR // 8, 8, TOK), axis=0)

    ssq = lax.fori_loop(0, NB, gate_step, jnp.zeros((8, TOK), F32))
    scale = lax.rsqrt(jnp.sum(ssq, axis=0, keepdims=True) * (1.0 / WIDTH) + EPS)

    def out_step(i, _):
        cols = pl.ds(pl.multiple_of(i * BR, BR), BR)
        v = (acc[cols, :] * scale).T
        out[:, cols] = (v * ng[:, cols]).astype(BF16)
        return 0

    lax.fori_loop(0, NB, out_step, 0)

    halo_copy.wait_send()
    th_copy.wait_send()

    def e_done(i, _):
        e_copy(i).wait_send()
        return 0

    lax.fori_loop(0, NB, e_done, 0)

    def drain(i, _):
        def dec_or_state(s, ss):
            dst = lbuf.at[0, chunk(i)]
            rcopy(dst, dst, ss.at[s, i], rsem.at[s, i], sib).wait_send()

        @pl.when(is_even)
        def _():
            dec_or_state(L1, ssem)

        @pl.when(jnp.logical_or(z4 == 1, z4 == 2))
        def _():
            dec_or_state(L2, ssem)

        @pl.when((z == 3) | (z == 4) | (z == 0) | (z == 7))
        def _():
            dec_or_state(L3, ssem)

        @pl.when(z == 3)
        def _():
            dec_or_state(L3, ssem2)

        @pl.when(jnp.logical_and(x < NX - 1, (z != 3) & (z != 4)))
        def _():
            dec_or_state(TT, ssem)

        @pl.when(jnp.logical_and(x < NX - 1, z == 7))
        def _():
            dec_or_state(TT, ssem2)

        @pl.when(jnp.logical_not(x_odd))
        def _():
            dec_or_state(X4, ssem)

        @pl.when(x <= 1)
        def _():
            dec_or_state(X5, ssem)

        @pl.when(x == 1)
        def _():
            dec_or_state(X5, ssem2)

        def sib_done(s):
            dst = lbuf.at[0, chunk(i)]
            rcopy(dst, dst, sib_s.at[s, i], sib_r.at[s, i], sib).wait_send()

        @pl.when(jnp.logical_not(is_even))
        def _():
            sib_done(L1)

        @pl.when(z4 >= 2)
        def _():
            sib_done(L2)

        @pl.when(z >= 4)
        def _():
            sib_done(L3)

        @pl.when(x_odd)
        def _():
            sib_done(X4)

        @pl.when(x >= 2)
        def _():
            sib_done(X5)

        return 0

    lax.fori_loop(0, NC, drain, 0)

    def ddone(s, ss):
        dcopy(dec.at[0], 0, s, sib, ss).wait_send()

    @pl.when(is_even)
    def _():
        ddone(L1, ssem)

    @pl.when(jnp.logical_or(z4 == 1, z4 == 2))
    def _():
        ddone(L2, ssem)

    @pl.when((z == 3) | (z == 4) | (z == 0) | (z == 7))
    def _():
        ddone(L3, ssem)

    @pl.when(z == 3)
    def _():
        ddone(L3, ssem2)

    @pl.when(jnp.logical_and(x < NX - 1, (z != 3) & (z != 4)))
    def _():
        ddone(TT, ssem)

    @pl.when(jnp.logical_and(x < NX - 1, z == 7))
    def _():
        ddone(TT, ssem2)

    @pl.when(jnp.logical_not(x_odd))
    def _():
        ddone(X4, ssem)


def per_device(
    mixed_input,
    conv_weight,
    conv_bias,
    gate_input,
    log_decay,
    level_weights,
    skip_gain,
    norm_gain,
    seg_lengths,
):
    vmem = pl.BlockSpec(memory_space=pltpu.VMEM)
    smem = pl.BlockSpec(memory_space=pltpu.SMEM)
    dma = pltpu.SemaphoreType.DMA
    return pl.pallas_call(
        kernel,
        out_shape=jax.ShapeDtypeStruct((TOK, WIDTH), BF16),
        in_specs=[vmem] * 7 + [smem] * 2,
        out_specs=vmem,
        scratch_shapes=[
            pltpu.VMEM((HALO, CH), BF16),
            pltpu.VMEM((TOK + 8, BR), F32),
            pltpu.VMEM((WIDTH, TOK), BF16),
            pltpu.VMEM((TOK, STATE), BF16),
            pltpu.VMEM((TOK, STATE), BF16),
            pltpu.VMEM((WIDTH, STATE), F32),
            pltpu.VMEM((WIDTH, STATE), F32),
            pltpu.VMEM((HALF, STATE), F32),
            pltpu.VMEM((4, NC, XR, STATE), jnp.int16),
            pltpu.VMEM((5, 2 * NC, XR, STATE), jnp.int16),
            pltpu.VMEM((NC, XR, STATE), jnp.int16),
            pltpu.VMEM((5, HEADS, 128), F32),
            pltpu.VMEM((3, HEADS, 128), F32),
            pltpu.VMEM((2, HEADS, 128), F32),
            pltpu.VMEM((6, HEADS, 128), F32),
            pltpu.VMEM((HEADS, TOK), F32),
            pltpu.VMEM((TOK, 128), F32),
            pltpu.VMEM((HEADS, TOK), F32),
            pltpu.VMEM((HEADS, TOK), F32),
            pltpu.VMEM((TOK, TOK), F32),
            pltpu.VMEM((128, 128), jnp.int32),
            pltpu.VMEM((WIDTH, TOK), F32),
            pltpu.VMEM((WIDTH, TOK), F32),
            dma,
            dma,
            dma,
            dma,
            dma((NB,)),
            dma((NB,)),
            dma((6, NC + 1)),
            dma((6, NC + 1)),
            dma((6, NC + 1)),
            dma((6, NC)),
            dma((6, NC)),
        ],
        compiler_params=pltpu.CompilerParams(
            collective_id=0, has_side_effects=True, vmem_limit_bytes=60 * 1024 * 1024
        ),
        name="layer",
    )(
        mixed_input,
        gate_input,
        log_decay,
        level_weights,
        conv_weight,
        conv_bias.reshape(1, CH),
        norm_gain.reshape(1, WIDTH),
        skip_gain,
        seg_lengths,
    )


def solution(mesh):
    in_specs = (
        P(("batch", "group"), None),
        P(),
        P(),
        P(("batch", "group"), None),
        P(None, ("batch", "group")),
        P(None, None, ("batch", "group")),
        P(),
        P(),
        P("batch"),
    )
    out_specs = P(("batch", "group"), None)
    return jax.shard_map(
        per_device, mesh=mesh, in_specs=in_specs, out_specs=out_specs, check_vma=False
    )
```

```python
import jax
import jax.numpy as jnp
from jax import lax
from jax.experimental import pallas as pl
from jax.experimental.pallas import tpu as pltpu
from jax.sharding import PartitionSpec as P

EPS = 1e-05
F32 = jnp.float32
BF16 = jnp.bfloat16
MESH = pl.DeviceIdType.MESH

TOK = 256
WIDTH = 2560
HEADS = 40
HD = 64
STATE = 128
CH = 2816
TAPS = 4
NX, NZ = 4, 8
HALF = WIDTH // 2
HALO = 16
PR = HALF // NZ
SG = 32
NSG = PR // SG
XP = PR + 16
PB = 2 * PR
NPB = WIDTH // PB
BR = 256
NB = WIDTH // BR
HPB = BR // HD
LOCAL_A = 8


def kernel(
    mixed_h,
    gate_h,
    ld,
    lam_h,
    cw,
    cb,
    ng,
    skip,
    segl,
    out,
    mixed,
    gate,
    lam,
    halo,
    pad,
    xst,
    keys,
    quer,
    ef,
    sibe,
    p1s,
    p1r,
    osnd,
    tr,
    lbuf,
    dtab,
    dline,
    theta,
    pbuf,
    cum,
    cumt,
    endw,
    entry,
    sct,
    lev,
    acc,
    gt,
    in_s,
    halo_s,
    halo_r,
    th_s,
    th_r,
    e_s,
    e_r,
    dz_s,
    dz_r,
    dx_s,
    dx_r,
    p1_s,
    p1_r,
    l_s,
    l_r,
    x_s,
    x_r,
    sib_s,
    sib_r,
):
    g = lax.axis_index("group")
    core = lax.rem(g, 2)
    z = lax.rem(g // 2, NZ)
    x = g // (2 * NZ)
    ngroups = 2 * NZ * NX

    def at(xx, zz, cc):
        return (xx * NZ + zz) * 2 + cc

    sib = at(x, z, 1 - core)
    gnext = lax.rem(g + 1, ngroups)
    gprev = lax.rem(g + ngroups - 1, ngroups)

    def zpeer(d):
        return lax.rem(z + d, NZ)

    def xpeer(d):
        return lax.rem(x + d, NX)

    barrier = pltpu.get_barrier_semaphore()

    def hello(peer):
        pl.semaphore_signal(barrier, inc=1, device_id={"group": peer}, device_id_type=MESH)

    for d in range(1, NZ):
        hello(at(x, zpeer(d), core))
    for d in range(1, NX):
        hello(at(xpeer(d), z, core))
    for peer in (sib, gnext, gprev):
        hello(peer)
    n_hello = NZ - 1 + NX - 1 + 3

    in_copies = [
        pltpu.make_async_copy(mixed_h, mixed, in_s.at[0]),
        pltpu.make_async_copy(lam_h, lam, in_s.at[1]),
        pltpu.make_async_copy(gate_h, gate, in_s.at[2]),
    ]
    for cp in in_copies:
        cp.start()

    def rcopy(src, dst, ss, rs, peer):
        return pltpu.make_async_remote_copy(
            src_ref=src,
            dst_ref=dst,
            send_sem=ss,
            recv_sem=rs,
            device_id={"group": peer},
            device_id_type=MESH,
        )

    first = g * TOK
    b1 = segl[0]
    b2 = segl[0] + segl[1]

    def seg_of(pos):
        s = (pos >= b1).astype(jnp.int32) + (pos >= b2).astype(jnp.int32)
        return jnp.where(pos >= 0, s, -1)

    lane_pos = first + lax.broadcasted_iota(jnp.int32, (8, TOK), 1)[0:1]
    seg_row = seg_of(lane_pos)
    last_row = seg_of(jnp.full((1, TOK), first + TOK - 1, jnp.int32))
    prev_row = seg_of(jnp.full((1, TOK), first - 1, jnp.int32))

    c = ld[...]
    lane = lax.broadcasted_iota(jnp.int32, (HEADS, TOK), 1)
    step = 1
    while step < TOK:
        c = c + jnp.where(lane >= step, pltpu.roll(c, step, 1), 0.0)
        step *= 2
    cum[...] = c
    c_end = c[:, TOK - 1 : TOK]
    endw[...] = jnp.exp(c_end - c) * (seg_row == last_row).astype(F32)
    entry[...] = jnp.exp(c) * (seg_row == prev_row).astype(F32)
    theta[0] = jnp.broadcast_to(jnp.exp(c_end), (HEADS, 128)) * (last_row == prev_row).astype(F32)[
        :, 0:128
    ]
    cpad = jnp.concatenate([c, jnp.zeros((128 - HEADS, TOK), F32)], axis=0)
    cumt[...] = jnp.concatenate([cpad[:, 0:128].T, cpad[:, 128:256].T], axis=0)

    si = lax.broadcasted_iota(jnp.int32, (128, 128), 0)
    ti = lax.broadcasted_iota(jnp.int32, (128, 128), 1)
    diff = si ^ ti
    lv = jnp.zeros((128, 128), jnp.int32)
    for b in range(7):
        lv = lv + (diff >= 2**b).astype(jnp.int32)
    lev[...] = lv

    in_copies[0].wait()
    pl.semaphore_wait(barrier, n_hello)

    halo_copy = rcopy(mixed.at[pl.ds(TOK - HALO, HALO)], halo, halo_s, halo_r, gnext)
    halo_copy.start()
    th_copy = rcopy(theta.at[0], theta.at[1], th_s, th_r, sib)
    th_copy.start()

    col_pos = first + lax.broadcasted_iota(jnp.int32, (TOK, 256), 0)
    seg_col = seg_of(col_pos)
    same = [None] + [seg_of(col_pos - t) == seg_col for t in range(1, TAPS)]

    def conv(cols):
        cur = mixed[:, cols].astype(F32)
        pad[8 : 8 + TOK, :] = cur
        pad[0:8, :] = halo[HALO - 8 : HALO, cols].astype(F32)
        total = cb[cols].reshape(1, BR) + cw[0:1, cols] * cur
        for t in range(1, TAPS):
            piece = pad[8 - t : 8 - t + TOK, :]
            total = total + cw[t : t + 1, cols] * jnp.where(same[t], piece, 0.0)
        return total * (1.0 / (1.0 + jnp.exp(-total)))

    halo_copy.wait_recv()
    kq = conv(pl.ds(WIDTH, 2 * STATE))
    keys[...] = kq[:, 0:STATE].astype(BF16)
    quer[...] = kq[:, STATE : 2 * STATE].astype(BF16)

    th_copy.wait_recv()
    dtab[z] = theta[0] * theta[1]

    def dz_copy(to, frm):
        return rcopy(dtab.at[frm], dtab.at[frm], dz_s.at[to], dz_r.at[frm], at(x, to, core))

    def dx_copy(to, frm):
        return rcopy(dline.at[frm], dline.at[frm], dx_s.at[to], dx_r.at[frm], at(to, z, core))

    def over_z(f):
        def go(d, _):
            f(zpeer(d))
            return 0

        lax.fori_loop(1, NZ, go, 0)

    def over_x(f):
        def go(d, _):
            f(xpeer(d))
            return 0

        lax.fori_loop(1, NX, go, 0)

    over_z(lambda o: dz_copy(o, z).start())

    def e_copy(i):
        rows = pl.ds(pl.multiple_of(i * BR, BR), BR)
        return rcopy(ef.at[rows], sibe.at[rows], e_s.at[i], e_r.at[i], sib)

    def conv_step(n, _):
        i = lax.rem(n + (1 - core) * (NB // 2), NB)
        base = pl.multiple_of(i * BR, BR)
        act = conv(pl.ds(base, BR)).T.astype(BF16)
        xst[pl.ds(base, BR), :] = act
        parts = []
        for j in range(HPB):
            w = endw[pl.ds(i * HPB + j, 1), :]
            parts.append((act[j * HD : (j + 1) * HD].astype(F32) * w).astype(BF16))
        e = jnp.dot(jnp.concatenate(parts, axis=0), keys[...], preferred_element_type=F32)
        ef[pl.ds(base, BR), :] = e
        e_copy(i).start()
        return 0

    lax.fori_loop(0, NB, conv_step, 0)

    xrow = lax.broadcasted_iota(jnp.int32, (16, 128), 0) // 3

    def encode(blocks):
        q = []
        ex = jnp.zeros((16, 128), F32)
        for k in range(NSG):
            top = jnp.max(jnp.abs(blocks[k]), axis=0, keepdims=True)
            e = jnp.ceil(jnp.log2(jnp.maximum(top, 1e-30))) - 14.0
            q.append(jnp.floor(blocks[k] * (1.0 / jnp.exp2(e)) + 0.5))
            ex = jnp.where(xrow == k, e, ex)
        return jnp.concatenate(q + [ex], axis=0).astype(jnp.int32).astype(jnp.int16)

    def decode(ref):
        ex = jnp.exp2(ref[PR:XP, :].astype(jnp.int32).astype(F32))
        return [
            ref[k * SG : (k + 1) * SG, :].astype(jnp.int32).astype(F32) * ex[3 * k : 3 * k + 1]
            for k in range(NSG)
        ]

    def head_of(o, k):
        return core * (HEADS // 2) + (o * NSG + k) // 2

    def p1_copy(to, frm):
        return rcopy(p1s.at[to], p1r.at[frm], p1_s.at[to], p1_r.at[frm], at(x, to, core))

    def wait_e(n, _):
        e_copy(core * (NB // 2) + n).wait_recv()
        return 0

    lax.fori_loop(0, NB // 2, wait_e, 0)

    def chip_step(n, _):
        o = lax.rem(z + NZ // 2 + n, NZ)
        blocks = []
        for k in range(NSG):
            rows = pl.ds(pl.multiple_of(core * HALF + o * PR + k * SG, SG), SG)
            own, other = ef[rows, :], sibe[rows, :]
            h = pl.ds(head_of(o, k), 1)
            low = jnp.where(core == 0, own, other)
            high = jnp.where(core == 0, other, own)
            d = jnp.where(core == 0, theta[1, h, :], theta[0, h, :])
            blocks.append(low * d + high)
        p1s[o] = encode(blocks)

        @pl.when(o != z)
        def _():
            p1_copy(o, z).start()

        @pl.when(o == z)
        def _():
            p1r[o] = p1s[o]

        return 0

    lax.fori_loop(0, NZ, chip_step, 0)

    over_z(lambda o: dz_copy(o, o).wait_recv())
    pair = [dtab[2 * j] * dtab[2 * j + 1] for j in range(NZ // 2)]
    quad = [pair[0] * pair[1], pair[2] * pair[3]]
    dline[x] = quad[0] * quad[1]
    over_x(lambda o: dx_copy(o, x).start())
    one = jnp.ones((HEADS, 128), F32)
    pbuf[1] = jnp.where(core == 1, theta[1], one)
    below = jnp.where(lax.rem(z, 2) == 1, dtab[jnp.maximum(z - 1, 0)], one)
    pbuf[2] = pbuf[1] * below
    pbuf[3] = pbuf[2] * jnp.where(
        lax.rem(z // 2, 2) == 1, jnp.where(z >= 4, pair[2], pair[0]), one
    )
    pbuf[4] = pbuf[3] * jnp.where(z >= 4, quad[0], one)

    s_t = lax.dot_general(
        keys[...], quer[...], (((1,), (1,)), ((), ())), preferred_element_type=F32
    )
    rowi = lax.broadcasted_iota(jnp.int32, (TOK, TOK), 0)
    coli = lax.broadcasted_iota(jnp.int32, (TOK, TOK), 1)
    ok = (rowi <= coli) & (seg_col == seg_row)
    sct[...] = jnp.where(ok, s_t, 0.0)

    def local_heads(i, _):
        rolled = pltpu.roll(cumt[...], lax.rem(128 - i * HPB, 128), 1)
        for j in range(HPB):
            h = i * HPB + j
            rows = pl.ds(pl.multiple_of(h * HD, HD), HD)
            ccol = rolled[:, j : j + 1]
            crow = cum[pl.ds(h, 1), :]

            def lam_row(l, lo):
                return lam[l, pl.ds(h, 1), :][:, lo : lo + 128]

            def picked(lo):
                p = jnp.broadcast_to(lam_row(7, lo), (128, 128))
                for l in range(7):
                    p = jnp.where(lev[...] == l, lam_row(l, lo), p)
                return p

            def mix(slo, tlo, pick):
                gap = crow[:, tlo : tlo + 128] - ccol[slo : slo + 128]
                decay = jnp.exp(jnp.minimum(gap, 0.0))
                return (sct[slo : slo + 128, tlo : tlo + 128] * pick * decay).astype(BF16)

            m00 = mix(0, 0, picked(0))
            m01 = mix(0, 128, lam_row(8, 128))
            m11 = mix(128, 128, picked(128))
            xs = xst[rows, :]
            left = jnp.dot(xs[:, 0:128], m00, preferred_element_type=F32)
            right = jnp.dot(xs, jnp.concatenate([m01, m11], axis=0), preferred_element_type=F32)
            acc[rows, :] = jnp.concatenate([left, right], axis=1) + skip[h] * xs.astype(F32)
        return 0

    in_copies[1].wait()
    lax.fori_loop(0, LOCAL_A, local_heads, 0)

    over_z(lambda o: p1_copy(o, o).wait_recv())
    cs = [decode(p1r.at[j]) for j in range(NZ)]
    b01, b45, b03, b07 = [], [], [], []
    for k in range(NSG):
        h = pl.ds(head_of(z, k), 1)
        d = [dtab[j, h, :] for j in range(NZ)]
        pr = [cs[2 * j][k] * d[2 * j + 1] + cs[2 * j + 1][k] for j in range(NZ // 2)]
        lo = pr[0] * (d[2] * d[3]) + pr[1]
        hi = pr[2] * (d[6] * d[7]) + pr[3]
        b01.append(pr[0])
        b45.append(pr[2])
        b03.append(lo)
        b07.append(lo * (d[4] * d[5] * d[6] * d[7]) + hi)
    osnd[3] = encode(b07)

    def x_copy(to, frm):
        return rcopy(osnd.at[3], tr.at[frm], x_s.at[to], x_r.at[frm], at(to, z, core))

    def send_x(o):
        @pl.when(o > x)
        def _():
            x_copy(o, x).start()

    over_x(send_x)
    osnd[2] = encode(b03)
    osnd[0] = encode(b01)
    osnd[1] = encode(b45)

    me = core * NZ + z

    def l_copy(lvl, src, o, frm):
        return rcopy(
            src, lbuf.at[lvl, core * NZ + frm], l_s.at[lvl, o], l_r.at[lvl, frm], at(x, o, core)
        )

    def sib_copy(lvl, o):
        dst = lbuf.at[lvl, core * NZ + o]
        return rcopy(dst, dst, sib_s.at[lvl, o], sib_r.at[lvl, o], sib)

    def sib_wait(lvl, o):
        dst = lbuf.at[lvl, (1 - core) * NZ + o]
        rcopy(dst, dst, sib_s.at[lvl, o], sib_r.at[lvl, o], sib).wait_recv()

    def bit(v, b):
        return lax.rem(v // 2**b, 2) == 1

    def keep(lvl, src):
        lbuf[lvl, me] = src
        sib_copy(lvl, z).start()

    def send_l3(o):
        @pl.when(o >= 4)
        def _():
            l_copy(2, osnd.at[2], o, z).start()

    def send_l2(o):
        @pl.when(bit(o, 1))
        def _():
            l_copy(1, osnd.at[o // 4], o, z).start()

    over_z(send_l3)
    over_z(send_l2)

    def l1_copy(o):
        return rcopy(
            p1s.at[o],
            lbuf.at[0, core * NZ + o],
            l_s.at[0, o],
            l_r.at[0, o],
            at(x, zpeer(1), core),
        )

    def send_l1(o, _):
        l1_copy(o).start()
        return 0

    @pl.when(lax.rem(z, 2) == 0)
    def _():
        lax.fori_loop(0, NZ, send_l1, 0)

    @pl.when(z >= 4)
    def _():
        keep(2, osnd[2])

    @pl.when(bit(z, 1))
    def _():
        keep(1, osnd[z // 4])

    lax.fori_loop(LOCAL_A, NB, local_heads, 0)

    over_x(lambda o: dx_copy(o, o).wait_recv())
    pbuf[5] = pbuf[4] * jnp.where(lax.rem(x, 2) == 1, dline[jnp.maximum(x - 1, 0)], one)

    def x_in(frm):
        x_copy(frm, frm).wait_recv()

    def send_l4(frm):
        over_z(lambda o: l_copy(3, tr.at[frm], o, z).start())
        keep(3, tr[frm])

    def send_l5():
        t0, t1 = decode(tr.at[0]), decode(tr.at[1])
        osnd[4] = encode(
            [t0[k] * dline[1, pl.ds(head_of(z, k), 1), :] + t1[k] for k in range(NSG)]
        )
        over_z(lambda o: l_copy(4, osnd.at[4], o, z).start())
        keep(4, osnd[4])

    @pl.when(x == 1)
    def _():
        x_in(0)
        send_l4(0)

    @pl.when(x == 3)
    def _():
        x_in(2)
        send_l4(2)

    @pl.when(x >= 2)
    def _():
        x_in(1)
        x_in(0)
        send_l5()

    def pass_on(lvl):
        def one_piece(o):
            l_copy(lvl, lbuf.at[lvl, me], o, o).wait_recv()
            sib_copy(lvl, o).start()

        over_z(one_piece)

    def sib_all(lvl):
        def go(o, _):
            sib_wait(lvl, o)
            return 0

        lax.fori_loop(0, NZ, go, 0)

    def far(level):
        def body(i, _):
            base = pl.multiple_of(i * PB, PB)
            if level == 0:
                state = sibe[pl.ds(base, PB), :].astype(BF16)
            else:
                parts = []
                for m in range(2):
                    v = decode(lbuf.at[level - 1, 2 * i + m])
                    for k in range(NSG):
                        p = pbuf[level, pl.ds(i * NSG + (m * NSG + k) // 2, 1), :]
                        parts.append((v[k] * p).astype(BF16))
                state = jnp.concatenate(parts, axis=0)
            read = lax.dot_general(
                state, quer[...], (((1,), (1,)), ((), ())), preferred_element_type=F32
            )
            for j in range(NSG):
                h = pl.ds(i * NSG + j, 1)
                coef = lam[9 + level, h, :] * entry[h, :]
                rows = pl.ds(pl.multiple_of(base + j * HD, HD), HD)
                acc[rows, :] = acc[rows, :] + read[j * HD : (j + 1) * HD] * coef
            return 0

        lax.fori_loop(0, NPB, body, 0)

    def gate_block(i, _):
        cols = pl.ds(pl.multiple_of(i * BR, BR), BR)
        v = gate[:, cols].astype(F32)
        gt[cols, :] = (v * (1.0 / (1.0 + jnp.exp(-v)))).T
        return 0

    in_copies[2].wait()
    lax.fori_loop(0, NB, gate_block, 0)

    def wait_e2(n, _):
        e_copy((1 - core) * (NB // 2) + n).wait_recv()
        return 0

    lax.fori_loop(0, NB // 2, wait_e2, 0)

    @pl.when(core == 1)
    def _():
        far(0)

    @pl.when(z >= 4)
    def _():
        pass_on(2)

    @pl.when(bit(z, 1))
    def _():
        pass_on(1)

    @pl.when(lax.rem(z, 2) == 1)
    def _():
        def go(o, _):
            l1_copy(o).wait_recv()
            sib_copy(0, o).start()
            return 0

        lax.fori_loop(0, NZ, go, 0)

    @pl.when(z >= 4)
    def _():
        sib_all(2)
        far(3)

    @pl.when(bit(z, 1))
    def _():
        sib_all(1)
        far(2)

    @pl.when(lax.rem(z, 2) == 1)
    def _():
        sib_all(0)
        far(1)

    @pl.when(lax.rem(x, 2) == 1)
    def _():
        pass_on(3)

    @pl.when(x >= 2)
    def _():
        pass_on(4)

    @pl.when(lax.rem(x, 2) == 1)
    def _():
        sib_all(3)
        far(4)

    @pl.when(x >= 2)
    def _():
        sib_all(4)
        far(5)

    def gate_step(i, ssq):
        rows = pl.ds(pl.multiple_of(i * BR, BR), BR)
        v = acc[rows, :] * gt[rows, :]
        acc[rows, :] = v
        return ssq + jnp.sum((v * v).reshape(BR // 8, 8, TOK), axis=0)

    ssq = lax.fori_loop(0, NB, gate_step, jnp.zeros((8, TOK), F32))
    scale = lax.rsqrt(jnp.sum(ssq, axis=0, keepdims=True) * (1.0 / WIDTH) + EPS)

    def out_step(i, _):
        cols = pl.ds(pl.multiple_of(i * BR, BR), BR)
        v = (acc[cols, :] * scale).T
        out[:, cols] = (v * ng[cols].reshape(1, BR)).astype(BF16)
        return 0

    lax.fori_loop(0, NB, out_step, 0)

    halo_copy.wait_send()
    th_copy.wait_send()

    def e_done(i, _):
        e_copy(i).wait_send()
        return 0

    lax.fori_loop(0, NB, e_done, 0)
    over_z(lambda o: dz_copy(o, z).wait_send())
    over_z(lambda o: p1_copy(o, z).wait_send())
    over_x(lambda o: dx_copy(o, x).wait_send())

    def x_done(o):
        @pl.when(o > x)
        def _():
            x_copy(o, x).wait_send()

    over_x(x_done)

    def l_done(o):
        @pl.when(o >= 4)
        def _():
            l_copy(2, osnd.at[2], o, z).wait_send()

        @pl.when(bit(o, 1))
        def _():
            l_copy(1, osnd.at[0], o, z).wait_send()

        @pl.when(lax.rem(x, 2) == 1)
        def _():
            l_copy(3, tr.at[0], o, z).wait_send()

        @pl.when(x >= 2)
        def _():
            l_copy(4, osnd.at[4], o, z).wait_send()

    over_z(l_done)

    def sib_done(lvl):
        def go(o, _):
            sib_copy(lvl, o).wait_send()
            return 0

        lax.fori_loop(0, NZ, go, 0)

    @pl.when(lax.rem(z, 2) == 0)
    def _():
        def go(o, _):
            l1_copy(o).wait_send()
            return 0

        lax.fori_loop(0, NZ, go, 0)

    pl.when(lax.rem(z, 2) == 1)(lambda: sib_done(0))
    pl.when(bit(z, 1))(lambda: sib_done(1))
    pl.when(z >= 4)(lambda: sib_done(2))
    pl.when(lax.rem(x, 2) == 1)(lambda: sib_done(3))
    pl.when(x >= 2)(lambda: sib_done(4))


def per_device(
    mixed_input,
    conv_weight,
    conv_bias,
    gate_input,
    log_decay,
    level_weights,
    skip_gain,
    norm_gain,
    seg_lengths,
):
    vmem = pl.BlockSpec(memory_space=pltpu.VMEM)
    hbm = pl.BlockSpec(memory_space=pl.ANY)
    smem = pl.BlockSpec(memory_space=pltpu.SMEM)
    dma = pltpu.SemaphoreType.DMA
    return pl.pallas_call(
        kernel,
        out_shape=jax.ShapeDtypeStruct((TOK, WIDTH), BF16),
        in_specs=[hbm, hbm, vmem, hbm] + [vmem] * 3 + [smem] * 2,
        out_specs=vmem,
        scratch_shapes=[
            pltpu.VMEM((TOK, CH), BF16),
            pltpu.VMEM((TOK, WIDTH), BF16),
            pltpu.VMEM((20, HEADS, TOK), F32),
            pltpu.VMEM((HALO, CH), BF16),
            pltpu.VMEM((TOK + 8, BR), F32),
            pltpu.VMEM((WIDTH, TOK), BF16),
            pltpu.VMEM((TOK, STATE), BF16),
            pltpu.VMEM((TOK, STATE), BF16),
            pltpu.VMEM((WIDTH, STATE), F32),
            pltpu.VMEM((WIDTH, STATE), F32),
            pltpu.VMEM((NZ, XP, STATE), jnp.int16),
            pltpu.VMEM((NZ, XP, STATE), jnp.int16),
            pltpu.VMEM((5, XP, STATE), jnp.int16),
            pltpu.VMEM((NX, XP, STATE), jnp.int16),
            pltpu.VMEM((5, 2 * NZ, XP, STATE), jnp.int16),
            pltpu.VMEM((NZ, HEADS, 128), F32),
            pltpu.VMEM((NX, HEADS, 128), F32),
            pltpu.VMEM((2, HEADS, 128), F32),
            pltpu.VMEM((6, HEADS, 128), F32),
            pltpu.VMEM((HEADS, TOK), F32),
            pltpu.VMEM((TOK, 128), F32),
            pltpu.VMEM((HEADS, TOK), F32),
            pltpu.VMEM((HEADS, TOK), F32),
            pltpu.VMEM((TOK, TOK), F32),
            pltpu.VMEM((128, 128), jnp.int32),
            pltpu.VMEM((WIDTH, TOK), F32),
            pltpu.VMEM((WIDTH, TOK), F32),
            dma((3,)),
            dma,
            dma,
            dma,
            dma,
            dma((NB,)),
            dma((NB,)),
            dma((NZ,)),
            dma((NZ,)),
            dma((NX,)),
            dma((NX,)),
            dma((NZ,)),
            dma((NZ,)),
            dma((5, NZ)),
            dma((5, NZ)),
            dma((NX,)),
            dma((NX,)),
            dma((5, NZ)),
            dma((5, NZ)),
        ],
        compiler_params=pltpu.CompilerParams(
            collective_id=0, has_side_effects=True, vmem_limit_bytes=60 * 1024 * 1024
        ),
        name="layer",
    )(
        mixed_input,
        gate_input,
        log_decay,
        jnp.transpose(level_weights, (1, 0, 2)),
        conv_weight,
        conv_bias,
        norm_gain,
        skip_gain,
        seg_lengths,
    )


def solution(mesh):
    in_specs = (
        P(("batch", "group"), None),
        P(),
        P(),
        P(("batch", "group"), None),
        P(None, ("batch", "group")),
        P(None, None, ("batch", "group")),
        P(),
        P(),
        P("batch"),
    )
    out_specs = P(("batch", "group"), None)
    return jax.shard_map(
        per_device, mesh=mesh, in_specs=in_specs, out_specs=out_specs, check_vma=False
    )
```

```python
import jax
import jax.numpy as jnp
from jax import lax
from jax.experimental import pallas as pl
from jax.experimental.pallas import tpu as pltpu
from jax.sharding import PartitionSpec as P

EPS = 1e-05
F32 = jnp.float32
BF16 = jnp.bfloat16
MESH = pl.DeviceIdType.MESH

TOK = 256
WIDTH = 2560
HEADS = 40
HD = 64
STATE = 128
CH = 2816
TAPS = 4
NX, NZ = 4, 8
HALF = WIDTH // 2
HALO = 16
PR = HALF // NZ
SG = 32
NSG = PR // SG
XP = PR + 16
PB = 2 * PR
NPB = WIDTH // PB
BR = 256
NB = WIDTH // BR
HPB = BR // HD
LOCAL_A = 8
CONV_A = 4


def kernel(
    mixed_h,
    gate_h,
    ld,
    lam_h,
    cw,
    cb,
    ng,
    skip,
    segl,
    out,
    mixed,
    gate,
    lam,
    halo,
    pad,
    act,
    xst,
    keys,
    quer,
    ef,
    sibe,
    p1s,
    p1r,
    osnd,
    tr,
    lbuf,
    dtab,
    dline,
    theta,
    pbuf,
    cum,
    cumt,
    endw,
    entry,
    sct,
    lev,
    acc,
    gt,
    in_s,
    halo_s,
    halo_r,
    th_s,
    th_r,
    e_s,
    e_r,
    dz_s,
    dz_r,
    dx_s,
    dx_r,
    p1_s,
    p1_r,
    l_s,
    l_r,
    r2_s,
    r3_s,
    r_s,
    up_s,
    x_s,
    x_r,
    sib_s,
    sib_r,
):
    g = lax.axis_index("group")
    core = lax.rem(g, 2)
    z = lax.rem(g // 2, NZ)
    x = g // (2 * NZ)
    ngroups = 2 * NZ * NX

    def at(xx, zz, cc):
        return (xx * NZ + zz) * 2 + cc

    sib = at(x, z, 1 - core)
    gnext = lax.rem(g + 1, ngroups)
    gprev = lax.rem(g + ngroups - 1, ngroups)

    def zpeer(d):
        return lax.rem(z + d, NZ)

    def xpeer(d):
        return lax.rem(x + d, NX)

    barrier = pltpu.get_barrier_semaphore()

    def hello(peer):
        pl.semaphore_signal(barrier, inc=1, device_id={"group": peer}, device_id_type=MESH)

    for d in range(1, NZ):
        hello(at(x, zpeer(d), core))
    for d in range(1, NX):
        hello(at(xpeer(d), z, core))
    for peer in (sib, gnext, gprev):
        hello(peer)
    n_hello = NZ - 1 + NX - 1 + 3

    in_copies = [
        pltpu.make_async_copy(mixed_h, mixed, in_s.at[0]),
        pltpu.make_async_copy(lam_h, lam, in_s.at[1]),
        pltpu.make_async_copy(gate_h, gate, in_s.at[2]),
    ]
    for cp in in_copies:
        cp.start()

    def rcopy(src, dst, ss, rs, peer):
        return pltpu.make_async_remote_copy(
            src_ref=src,
            dst_ref=dst,
            send_sem=ss,
            recv_sem=rs,
            device_id={"group": peer},
            device_id_type=MESH,
        )

    first = g * TOK
    b1 = segl[0]
    b2 = segl[0] + segl[1]

    def seg_of(pos):
        s = (pos >= b1).astype(jnp.int32) + (pos >= b2).astype(jnp.int32)
        return jnp.where(pos >= 0, s, -1)

    lane_pos = first + lax.broadcasted_iota(jnp.int32, (8, TOK), 1)[0:1]
    seg_row = seg_of(lane_pos)
    last_row = seg_of(jnp.full((1, TOK), first + TOK - 1, jnp.int32))
    prev_row = seg_of(jnp.full((1, TOK), first - 1, jnp.int32))

    c = ld[...]
    lane = lax.broadcasted_iota(jnp.int32, (HEADS, TOK), 1)
    step = 1
    while step < TOK:
        c = c + jnp.where(lane >= step, pltpu.roll(c, step, 1), 0.0)
        step *= 2
    cum[...] = c
    c_end = c[:, TOK - 1 : TOK]
    endw[...] = jnp.exp(c_end - c) * (seg_row == last_row).astype(F32)
    entry[...] = jnp.exp(c) * (seg_row == prev_row).astype(F32)
    theta[0] = jnp.broadcast_to(jnp.exp(c_end), (HEADS, 128)) * (last_row == prev_row).astype(F32)[
        :, 0:128
    ]
    cpad = jnp.concatenate([c, jnp.zeros((128 - HEADS, TOK), F32)], axis=0)
    cumt[...] = jnp.concatenate([cpad[:, 0:128].T, cpad[:, 128:256].T], axis=0)

    si = lax.broadcasted_iota(jnp.int32, (128, 128), 0)
    ti = lax.broadcasted_iota(jnp.int32, (128, 128), 1)
    diff = si ^ ti
    lv = jnp.zeros((128, 128), jnp.int32)
    for b in range(7):
        lv = lv + (diff >= 2**b).astype(jnp.int32)
    lev[...] = lv

    col_pos = first + lax.broadcasted_iota(jnp.int32, (TOK, 256), 0)
    seg_col = seg_of(col_pos)
    same = [None] + [seg_of(col_pos - t) == seg_col for t in range(1, TAPS)]

    def taps(cols, rows, cur):
        total = cb[cols].reshape(1, BR) + cw[0:1, cols] * cur
        for t in range(1, TAPS):
            piece = pad[8 - t : 8 - t + rows, :]
            total = total + cw[t : t + 1, cols] * jnp.where(same[t][0:rows], piece, 0.0)
        return total * (1.0 / (1.0 + jnp.exp(-total)))

    pad[0:8, :] = jnp.zeros((8, BR), F32)

    def conv_rows(i, _):
        cols = pl.ds(pl.multiple_of(i * BR, BR), BR)
        cur = mixed[:, cols].astype(F32)
        pad[8 : 8 + TOK, :] = cur
        act[:, cols] = taps(cols, TOK, cur)
        return 0

    def conv_first(i, _):
        cols = pl.ds(pl.multiple_of(i * BR, BR), BR)
        cur = mixed[0:16, cols].astype(F32)[0:8]
        pad[8:16, :] = cur
        pad[0:8, :] = halo[:, cols].astype(F32)[8:16]
        act[0:8, cols] = taps(cols, 8, cur)
        return 0

    in_copies[0].wait()
    lax.fori_loop(0, CONV_A, conv_rows, 0)
    pl.semaphore_wait(barrier, n_hello)

    halo_copy = rcopy(mixed.at[pl.ds(TOK - HALO, HALO)], halo, halo_s, halo_r, gnext)
    halo_copy.start()
    th_copy = rcopy(theta.at[0], theta.at[1], th_s, th_r, sib)
    th_copy.start()
    lax.fori_loop(CONV_A, CH // BR, conv_rows, 0)

    th_copy.wait_recv()
    dtab[z] = theta[0] * theta[1]

    def dz_copy(to, frm):
        return rcopy(dtab.at[frm], dtab.at[frm], dz_s.at[to], dz_r.at[frm], at(x, to, core))

    def dx_copy(to, frm):
        return rcopy(dline.at[frm], dline.at[frm], dx_s.at[to], dx_r.at[frm], at(to, z, core))

    def over_z(f):
        def go(d, _):
            f(zpeer(d))
            return 0

        lax.fori_loop(1, NZ, go, 0)

    def over_x(f):
        def go(d, _):
            f(xpeer(d))
            return 0

        lax.fori_loop(1, NX, go, 0)

    over_z(lambda o: dz_copy(o, z).start())

    halo_copy.wait_recv()
    lax.fori_loop(0, CH // BR, conv_first, 0)
    keys[...] = act[:, WIDTH : WIDTH + STATE].astype(BF16)
    quer[...] = act[:, WIDTH + STATE : CH].astype(BF16)

    def e_copy(i):
        rows = pl.ds(pl.multiple_of(i * BR, BR), BR)
        return rcopy(ef.at[rows], sibe.at[rows], e_s.at[i], e_r.at[i], sib)

    def conv_step(n, _):
        i = lax.rem(n + (1 - core) * (NB // 2), NB)
        base = pl.multiple_of(i * BR, BR)
        xt = act[:, pl.ds(base, BR)].T.astype(BF16)
        xst[pl.ds(base, BR), :] = xt
        parts = []
        for j in range(HPB):
            w = endw[pl.ds(i * HPB + j, 1), :]
            parts.append((xt[j * HD : (j + 1) * HD].astype(F32) * w).astype(BF16))
        e = jnp.dot(jnp.concatenate(parts, axis=0), keys[...], preferred_element_type=F32)
        ef[pl.ds(base, BR), :] = e
        e_copy(i).start()
        return 0

    lax.fori_loop(0, NB, conv_step, 0)

    xrow = lax.broadcasted_iota(jnp.int32, (16, 128), 0) // 3

    def encode(blocks):
        q = []
        ex = jnp.zeros((16, 128), F32)
        for k in range(NSG):
            top = jnp.max(jnp.abs(blocks[k]), axis=0, keepdims=True)
            e = jnp.ceil(jnp.log2(jnp.maximum(top, 1e-30))) - 14.0
            q.append(jnp.floor(blocks[k] * (1.0 / jnp.exp2(e)) + 0.5))
            ex = jnp.where(xrow == k, e, ex)
        return jnp.concatenate(q + [ex], axis=0).astype(jnp.int32).astype(jnp.int16)

    def decode(ref):
        ex = jnp.exp2(ref[PR:XP, :].astype(jnp.int32).astype(F32))
        return [
            ref[k * SG : (k + 1) * SG, :].astype(jnp.int32).astype(F32) * ex[3 * k : 3 * k + 1]
            for k in range(NSG)
        ]

    def head_of(o, k):
        return core * (HEADS // 2) + (o * NSG + k) // 2

    over_z(lambda o: dz_copy(o, o).wait_recv())
    pair = [dtab[2 * j] * dtab[2 * j + 1] for j in range(NZ // 2)]
    quad = [pair[0] * pair[1], pair[2] * pair[3]]
    dline[x] = quad[0] * quad[1]
    over_x(lambda o: dx_copy(o, x).start())

    def p1_copy(to, frm):
        return rcopy(p1s.at[to], p1r.at[frm], p1_s.at[to], p1_r.at[frm], at(x, to, core))

    def wait_e(n, _):
        e_copy(core * (NB // 2) + n).wait_recv()
        return 0

    lax.fori_loop(0, NB // 2, wait_e, 0)

    def chip_step(n, _):
        o = lax.rem(z + NZ // 2 + n, NZ)
        blocks = []
        for k in range(NSG):
            rows = pl.ds(pl.multiple_of(core * HALF + o * PR + k * SG, SG), SG)
            own, other = ef[rows, :], sibe[rows, :]
            h = pl.ds(head_of(o, k), 1)
            low = jnp.where(core == 0, own, other)
            high = jnp.where(core == 0, other, own)
            d = jnp.where(core == 0, theta[1, h, :], theta[0, h, :])
            blocks.append(low * d + high)
        p1s[o] = encode(blocks)

        @pl.when(o != z)
        def _():
            p1_copy(o, z).start()

        @pl.when(o == z)
        def _():
            p1r[o] = p1s[o]

        return 0

    lax.fori_loop(0, NZ, chip_step, 0)

    s_t = lax.dot_general(
        keys[...], quer[...], (((1,), (1,)), ((), ())), preferred_element_type=F32
    )
    rowi = lax.broadcasted_iota(jnp.int32, (TOK, TOK), 0)
    coli = lax.broadcasted_iota(jnp.int32, (TOK, TOK), 1)
    ok = (rowi <= coli) & (seg_col == seg_row)
    sct[...] = jnp.where(ok, s_t, 0.0)

    def local_heads(i, _):
        rolled = pltpu.roll(cumt[...], lax.rem(128 - i * HPB, 128), 1)
        for j in range(HPB):
            h = i * HPB + j
            rows = pl.ds(pl.multiple_of(h * HD, HD), HD)
            ccol = rolled[:, j : j + 1]
            crow = cum[pl.ds(h, 1), :]

            def lam_row(l, lo):
                return lam[l, pl.ds(h, 1), :][:, lo : lo + 128]

            def picked(lo):
                p = jnp.broadcast_to(lam_row(7, lo), (128, 128))
                for l in range(7):
                    p = jnp.where(lev[...] == l, lam_row(l, lo), p)
                return p

            def mix(slo, tlo, pick):
                gap = crow[:, tlo : tlo + 128] - ccol[slo : slo + 128]
                decay = jnp.exp(jnp.minimum(gap, 0.0))
                return (sct[slo : slo + 128, tlo : tlo + 128] * pick * decay).astype(BF16)

            m00 = mix(0, 0, picked(0))
            m01 = mix(0, 128, lam_row(8, 128))
            m11 = mix(128, 128, picked(128))
            xs = xst[rows, :]
            left = jnp.dot(xs[:, 0:128], m00, preferred_element_type=F32)
            right = jnp.dot(xs, jnp.concatenate([m01, m11], axis=0), preferred_element_type=F32)
            acc[rows, :] = jnp.concatenate([left, right], axis=1) + skip[h] * xs.astype(F32)
        return 0

    pair = [dtab[2 * j] * dtab[2 * j + 1] for j in range(NZ // 2)]
    quad = [pair[0] * pair[1], pair[2] * pair[3]]
    one = jnp.ones((HEADS, 128), F32)
    pbuf[1] = jnp.where(core == 1, theta[1], one)
    below = jnp.where(lax.rem(z, 2) == 1, dtab[jnp.maximum(z - 1, 0)], one)
    pbuf[2] = pbuf[1] * below
    pbuf[3] = pbuf[2] * jnp.where(
        lax.rem(z // 2, 2) == 1, jnp.where(z >= 4, pair[2], pair[0]), one
    )
    pbuf[4] = pbuf[3] * jnp.where(z >= 4, quad[0], one)

    in_copies[1].wait()
    lax.fori_loop(0, LOCAL_A, local_heads, 0)

    over_z(lambda o: p1_copy(o, o).wait_recv())
    cs = [decode(p1r.at[j]) for j in range(NZ)]
    b01, b45, b03, b07 = [], [], [], []
    for k in range(NSG):
        h = pl.ds(head_of(z, k), 1)
        d = [dtab[j, h, :] for j in range(NZ)]
        pr = [cs[2 * j][k] * d[2 * j + 1] + cs[2 * j + 1][k] for j in range(NZ // 2)]
        lo = pr[0] * (d[2] * d[3]) + pr[1]
        hi = pr[2] * (d[6] * d[7]) + pr[3]
        b01.append(pr[0])
        b45.append(pr[2])
        b03.append(lo)
        b07.append(lo * (d[4] * d[5] * d[6] * d[7]) + hi)
    osnd[3] = encode(b07)

    def x_copy(to, frm):
        return rcopy(osnd.at[3], tr.at[frm], x_s.at[to], x_r.at[frm], at(to, z, core))

    def x_to(o):
        return (o > x) & ((o < 3) | (x == 2))

    def send_x(o):
        @pl.when(x_to(o))
        def _():
            x_copy(o, x).start()

    over_x(send_x)
    osnd[2] = encode(b03)
    osnd[0] = encode(b01)
    osnd[1] = encode(b45)

    me = core * NZ + z

    def l_copy(lvl, src, o, frm):
        return rcopy(
            src, lbuf.at[lvl, core * NZ + frm], l_s.at[lvl, o], l_r.at[lvl, frm], at(x, o, core)
        )

    def sib_copy(lvl, o):
        dst = lbuf.at[lvl, core * NZ + o]
        return rcopy(dst, dst, sib_s.at[lvl, o], sib_r.at[lvl, o], sib)

    def sib_wait(lvl, o):
        dst = lbuf.at[lvl, (1 - core) * NZ + o]
        rcopy(dst, dst, sib_s.at[lvl, o], sib_r.at[lvl, o], sib).wait_recv()

    def bit(v, b):
        return lax.rem(v // 2**b, 2) == 1

    def keep(lvl, src):
        lbuf[lvl, me] = src
        sib_copy(lvl, z).start()

    def mir(o):
        return jnp.where(z >= 6, lax.rem(11 - o, NZ), o)

    l3_to = jnp.where(z >= 2, 4, 7)
    l3_end = (z == 4) | (z == 7)
    l3_mid = (z == 5) | (z == 6)

    def l3_own(do):
        @pl.when(z < 4)
        def _():
            do(lambda: l_copy(2, osnd.at[2], l3_to, z))

        @pl.when(z >= 4)
        def _():
            do(lambda: l_copy(2, osnd.at[2], jnp.where(l3_end, mir(5), mir(4)), z))
            do(lambda: l_copy(2, osnd.at[2], mir(6), z))

    def l3_on(slot, o, to):
        dst = lbuf.at[2, core * NZ + o]
        return rcopy(dst, dst, r3_s.at[slot, o], l_r.at[2, o], at(x, to, core))

    def l3_in(o):
        l_copy(2, lbuf.at[2, me], o, o).wait_recv()

    def l3_first():
        @pl.when(l3_end)
        def _():
            for q in (3, 2):
                o = mir(q)
                l3_in(o)
                l3_on(0, o, mir(5)).start()
                l3_on(1, o, mir(6)).start()
                sib_copy(2, o).start()

    def l3_rest():
        @pl.when(l3_mid)
        def _():
            for q in (6, 7, 0, 1):
                o = mir(q)
                l3_in(o)
                l3_on(0, o, mir(4)).start()
                sib_copy(2, o).start()
            for q in (4, 3, 2):
                o = mir(q)
                l3_in(o)
                sib_copy(2, o).start()

        @pl.when(l3_end)
        def _():
            for q in (5, 6, 7, 0, 1):
                o = mir(q)
                l3_in(o)
                sib_copy(2, o).start()

    def l3_on_done():
        @pl.when(l3_end)
        def _():
            for q in (3, 2):
                l3_on(0, mir(q), mir(5)).wait_send()
                l3_on(1, mir(q), mir(6)).wait_send()

        @pl.when(l3_mid)
        def _():
            for q in (6, 7, 0, 1):
                l3_on(0, mir(q), mir(4)).wait_send()

    def l2_own(do):
        for p in (2, 6):
            r = lax.rem(z + NZ - p, NZ)
            to = jnp.where((r == 1) | (r >= 5), p, p + 1)
            do(lambda to=to, p=p: l_copy(1, osnd.at[p // 4], to, z))

    l2_other = jnp.where(lax.rem(z, 2) == 0, z + 1, z - 1)

    def l2_off(d):
        return lax.rem(jnp.where(lax.rem(z, 2) == 0, z + NZ - d, z + d), NZ)

    def l2_on(o):
        dst = lbuf.at[1, core * NZ + o]
        return rcopy(dst, dst, r2_s.at[o], l_r.at[1, o], at(x, l2_other, core))

    def l2_in(o):
        l_copy(1, lbuf.at[1, me], o, o).wait_recv()

    def l2_first():
        @pl.when(bit(z, 1))
        def _():
            for d in (1, 2, 3):
                l2_in(l2_off(d))
                l2_on(l2_off(d)).start()
                sib_copy(1, l2_off(d)).start()

    def l2_rest():
        @pl.when(bit(z, 1))
        def _():
            for d in (7, 6, 5, 4):
                l2_in(l2_off(d))
                sib_copy(1, l2_off(d)).start()

    l3_own(lambda c: c().start())
    l2_own(lambda c: c().start())

    def l1_copy(o):
        return rcopy(
            p1s.at[o],
            lbuf.at[0, core * NZ + o],
            l_s.at[0, o],
            l_r.at[0, o],
            at(x, zpeer(1), core),
        )

    def send_l1(o, _):
        l1_copy(o).start()
        return 0

    @pl.when(lax.rem(z, 2) == 0)
    def _():
        lax.fori_loop(0, NZ, send_l1, 0)

    @pl.when(z >= 4)
    def _():
        keep(2, osnd[2])

    @pl.when(bit(z, 1))
    def _():
        keep(1, osnd[z // 4])

    def sib_all(lvl):
        def go(o, _):
            sib_wait(lvl, o)
            return 0

        lax.fori_loop(0, NZ, go, 0)

    def far(level):
        def body(i, _):
            base = pl.multiple_of(i * PB, PB)
            if level == 0:
                state = sibe[pl.ds(base, PB), :].astype(BF16)
            else:
                parts = []
                for m in range(2):
                    v = decode(lbuf.at[level - 1, 2 * i + m])
                    for k in range(NSG):
                        p = pbuf[level, pl.ds(i * NSG + (m * NSG + k) // 2, 1), :]
                        parts.append((v[k] * p).astype(BF16))
                state = jnp.concatenate(parts, axis=0)
            read = lax.dot_general(
                state, quer[...], (((1,), (1,)), ((), ())), preferred_element_type=F32
            )
            for j in range(NSG):
                h = pl.ds(i * NSG + j, 1)
                coef = lam[9 + level, h, :] * entry[h, :]
                rows = pl.ds(pl.multiple_of(base + j * HD, HD), HD)
                acc[rows, :] = acc[rows, :] + read[j * HD : (j + 1) * HD] * coef
            return 0

        lax.fori_loop(0, NPB, body, 0)

    def gate_block(i, _):
        cols = pl.ds(pl.multiple_of(i * BR, BR), BR)
        v = gate[:, cols].astype(F32)
        gt[cols, :] = (v * (1.0 / (1.0 + jnp.exp(-v)))).T
        return 0

    lax.fori_loop(LOCAL_A, NB, local_heads, 0)
    in_copies[2].wait()
    lax.fori_loop(0, NB, gate_block, 0)

    def wait_e2(n, _):
        e_copy((1 - core) * (NB // 2) + n).wait_recv()
        return 0

    lax.fori_loop(0, NB // 2, wait_e2, 0)

    @pl.when(core == 1)
    def _():
        far(0)

    over_x(lambda o: dx_copy(o, o).wait_recv())
    pbuf[5] = pbuf[4] * jnp.where(lax.rem(x, 2) == 1, dline[jnp.maximum(x - 1, 0)], one)

    def x_in(frm):
        x_copy(frm, frm).wait_recv()

    NEAR = (2, 6, 1, 7)

    def spread(lvl, src):
        for d in NEAR:
            l_copy(lvl, src, zpeer(d), z).start()

    def r_copy(lvl, d, frm):
        dst = lbuf.at[lvl, core * NZ + frm]
        to = zpeer(d)
        return rcopy(dst, dst, r_s.at[to], l_r.at[lvl, frm], at(x, to, core))

    z_odd = lax.rem(z, 2) == 1

    def up_copy(src, frm):
        return rcopy(
            src, lbuf.at[4, core * NZ + frm], up_s.at[frm], l_r.at[4, frm], at(xpeer(1), z, core)
        )

    def gather(lvl, up):
        def arrived(frm):
            l_copy(lvl, lbuf.at[lvl, me], frm, frm).wait_recv()

        def hand_on(frm):
            sib_copy(lvl, frm).start()
            if up:
                up_copy(lbuf.at[lvl, core * NZ + frm], frm).start()

        def pull(d):
            arrived(zpeer(d))
            hand_on(zpeer(d))

        arrived(zpeer(6))
        r_copy(lvl, 1, zpeer(6)).start()

        @pl.when(jnp.logical_not(z_odd))
        def _():
            r_copy(lvl, 2, zpeer(6)).start()

        hand_on(zpeer(6))
        arrived(zpeer(2))
        r_copy(lvl, 7, zpeer(2)).start()

        @pl.when(z_odd)
        def _():
            r_copy(lvl, 6, zpeer(2)).start()

        hand_on(zpeer(2))
        for d in (1, 7, 3, 5, 4):
            pull(d)

    def send_l4(frm):
        spread(3, tr.at[frm])
        keep(3, tr[frm])

    def send_l5():
        t0, t1 = decode(tr.at[0]), decode(tr.at[1])
        osnd[4] = encode(
            [t0[k] * dline[1, pl.ds(head_of(z, k), 1), :] + t1[k] for k in range(NSG)]
        )
        spread(4, osnd.at[4])
        up_copy(osnd.at[4], z).start()
        keep(4, osnd[4])

    @pl.when(x == 1)
    def _():
        x_in(0)
        send_l4(0)

    @pl.when(x == 3)
    def _():
        x_in(2)
        send_l4(2)

    @pl.when(x == 2)
    def _():
        x_in(1)
        x_in(0)
        send_l5()

    l3_first()
    l2_first()

    @pl.when(lax.rem(x, 2) == 1)
    def _():
        gather(3, False)

    @pl.when(x == 2)
    def _():
        gather(4, True)

    @pl.when(lax.rem(z, 2) == 1)
    def _():
        def go(o, _):
            l1_copy(o).wait_recv()
            sib_copy(0, o).start()
            return 0

        lax.fori_loop(0, NZ, go, 0)

    l3_rest()
    l2_rest()

    @pl.when(lax.rem(z, 2) == 1)
    def _():
        sib_all(0)
        far(1)

    @pl.when(bit(z, 1))
    def _():
        sib_all(1)
        far(2)

    @pl.when(z >= 4)
    def _():
        sib_all(2)
        far(3)

    @pl.when(x == 3)
    def _():
        def go(o, _):
            up_copy(osnd.at[4], o).wait_recv()
            sib_copy(4, o).start()
            return 0

        lax.fori_loop(0, NZ, go, 0)

    @pl.when(lax.rem(x, 2) == 1)
    def _():
        sib_all(3)
        far(4)

    @pl.when(x >= 2)
    def _():
        sib_all(4)
        far(5)

    def gate_step(i, ssq):
        rows = pl.ds(pl.multiple_of(i * BR, BR), BR)
        v = acc[rows, :] * gt[rows, :]
        acc[rows, :] = v
        return ssq + jnp.sum((v * v).reshape(BR // 8, 8, TOK), axis=0)

    ssq = lax.fori_loop(0, NB, gate_step, jnp.zeros((8, TOK), F32))
    scale = lax.rsqrt(jnp.sum(ssq, axis=0, keepdims=True) * (1.0 / WIDTH) + EPS)

    def out_step(i, _):
        cols = pl.ds(pl.multiple_of(i * BR, BR), BR)
        v = (acc[cols, :] * scale).T
        out[:, cols] = (v * ng[cols].reshape(1, BR)).astype(BF16)
        return 0

    lax.fori_loop(0, NB, out_step, 0)

    halo_copy.wait_send()
    th_copy.wait_send()

    def e_done(i, _):
        e_copy(i).wait_send()
        return 0

    lax.fori_loop(0, NB, e_done, 0)
    over_z(lambda o: dz_copy(o, z).wait_send())
    over_z(lambda o: p1_copy(o, z).wait_send())
    over_x(lambda o: dx_copy(o, x).wait_send())

    def x_done(o):
        @pl.when(x_to(o))
        def _():
            x_copy(o, x).wait_send()

    over_x(x_done)

    l3_own(lambda c: c().wait_send())
    l3_on_done()
    l2_own(lambda c: c().wait_send())

    @pl.when(bit(z, 1))
    def _():
        for d in (1, 2, 3):
            l2_on(l2_off(d)).wait_send()

    def spread_done(lvl):
        for d in NEAR:
            l_copy(lvl, osnd.at[4], zpeer(d), z).wait_send()
        for d in (1, 7):
            r_copy(lvl, d, z).wait_send()

        @pl.when(jnp.logical_not(z_odd))
        def _():
            r_copy(lvl, 2, z).wait_send()

        @pl.when(z_odd)
        def _():
            r_copy(lvl, 6, z).wait_send()

    pl.when(lax.rem(x, 2) == 1)(lambda: spread_done(3))

    @pl.when(x == 2)
    def _():
        spread_done(4)

        def go(o, _):
            up_copy(osnd.at[4], o).wait_send()
            return 0

        lax.fori_loop(0, NZ, go, 0)

    def sib_done(lvl):
        def go(o, _):
            sib_copy(lvl, o).wait_send()
            return 0

        lax.fori_loop(0, NZ, go, 0)

    @pl.when(lax.rem(z, 2) == 0)
    def _():
        def go(o, _):
            l1_copy(o).wait_send()
            return 0

        lax.fori_loop(0, NZ, go, 0)

    pl.when(lax.rem(z, 2) == 1)(lambda: sib_done(0))
    pl.when(bit(z, 1))(lambda: sib_done(1))
    pl.when(z >= 4)(lambda: sib_done(2))
    pl.when(lax.rem(x, 2) == 1)(lambda: sib_done(3))
    pl.when(x >= 2)(lambda: sib_done(4))


def per_device(
    mixed_input,
    conv_weight,
    conv_bias,
    gate_input,
    log_decay,
    level_weights,
    skip_gain,
    norm_gain,
    seg_lengths,
):
    vmem = pl.BlockSpec(memory_space=pltpu.VMEM)
    hbm = pl.BlockSpec(memory_space=pl.ANY)
    smem = pl.BlockSpec(memory_space=pltpu.SMEM)
    dma = pltpu.SemaphoreType.DMA
    return pl.pallas_call(
        kernel,
        out_shape=jax.ShapeDtypeStruct((TOK, WIDTH), BF16),
        in_specs=[hbm, hbm, vmem, hbm] + [vmem] * 3 + [smem] * 2,
        out_specs=vmem,
        scratch_shapes=[
            pltpu.VMEM((TOK, CH), BF16),
            pltpu.VMEM((TOK, WIDTH), BF16),
            pltpu.VMEM((20, HEADS, TOK), F32),
            pltpu.VMEM((HALO, CH), BF16),
            pltpu.VMEM((TOK + 8, BR), F32),
            pltpu.VMEM((TOK, CH), F32),
            pltpu.VMEM((WIDTH, TOK), BF16),
            pltpu.VMEM((TOK, STATE), BF16),
            pltpu.VMEM((TOK, STATE), BF16),
            pltpu.VMEM((WIDTH, STATE), F32),
            pltpu.VMEM((WIDTH, STATE), F32),
            pltpu.VMEM((NZ, XP, STATE), jnp.int16),
            pltpu.VMEM((NZ, XP, STATE), jnp.int16),
            pltpu.VMEM((5, XP, STATE), jnp.int16),
            pltpu.VMEM((NX, XP, STATE), jnp.int16),
            pltpu.VMEM((5, 2 * NZ, XP, STATE), jnp.int16),
            pltpu.VMEM((NZ, HEADS, 128), F32),
            pltpu.VMEM((NX, HEADS, 128), F32),
            pltpu.VMEM((2, HEADS, 128), F32),
            pltpu.VMEM((6, HEADS, 128), F32),
            pltpu.VMEM((HEADS, TOK), F32),
            pltpu.VMEM((TOK, 128), F32),
            pltpu.VMEM((HEADS, TOK), F32),
            pltpu.VMEM((HEADS, TOK), F32),
            pltpu.VMEM((TOK, TOK), F32),
            pltpu.VMEM((128, 128), jnp.int32),
            pltpu.VMEM((WIDTH, TOK), F32),
            pltpu.VMEM((WIDTH, TOK), F32),
            dma((3,)),
            dma,
            dma,
            dma,
            dma,
            dma((NB,)),
            dma((NB,)),
            dma((NZ,)),
            dma((NZ,)),
            dma((NX,)),
            dma((NX,)),
            dma((NZ,)),
            dma((NZ,)),
            dma((5, NZ)),
            dma((5, NZ)),
            dma((NZ,)),
            dma((2, NZ)),
            dma((NZ,)),
            dma((NZ,)),
            dma((NX,)),
            dma((NX,)),
            dma((5, NZ)),
            dma((5, NZ)),
        ],
        compiler_params=pltpu.CompilerParams(
            collective_id=0, has_side_effects=True, vmem_limit_bytes=60 * 1024 * 1024
        ),
        name="layer",
    )(
        mixed_input,
        gate_input,
        log_decay,
        jnp.transpose(level_weights, (1, 0, 2)),
        conv_weight,
        conv_bias,
        norm_gain,
        skip_gain,
        seg_lengths,
    )


def solution(mesh):
    in_specs = (
        P(("batch", "group"), None),
        P(),
        P(),
        P(("batch", "group"), None),
        P(None, ("batch", "group")),
        P(None, None, ("batch", "group")),
        P(),
        P(),
        P("batch"),
    )
    out_specs = P(("batch", "group"), None)
    return jax.shard_map(
        per_device, mesh=mesh, in_specs=in_specs, out_specs=out_specs, check_vma=False
    )
```

```python
import jax
import jax.numpy as jnp
from jax import lax
from jax.experimental import pallas as pl
from jax.experimental.pallas import tpu as pltpu
from jax.sharding import PartitionSpec as P

EPS = 1e-05
F32 = jnp.float32
BF16 = jnp.bfloat16
MESH = pl.DeviceIdType.MESH

TOK = 256
WIDTH = 2560
HEADS = 40
HD = 64
STATE = 128
CH = 2816
TAPS = 4
NX, NZ = 4, 8
HALF = WIDTH // 2
HALO = 16
PR = HALF // NZ
SG = 32
NSG = PR // SG
XP = PR + 16
PB = 2 * PR
NPB = WIDTH // PB
BR = 256
NB = WIDTH // BR
HPB = BR // HD
LOCAL_A = 8
CONV_A = 4


def kernel(
    mixed_h,
    gate_h,
    ld,
    lam_h,
    cw,
    cb,
    ng,
    skip,
    segl,
    out,
    mixed,
    gate,
    lam,
    halo,
    pad,
    act,
    xst,
    keys,
    quer,
    ef,
    sibe,
    p1s,
    p1r,
    osnd,
    tr,
    lbuf,
    dtab,
    dline,
    theta,
    pbuf,
    cum,
    cumt,
    endw,
    entry,
    sct,
    lev,
    acc,
    gt,
    in_s,
    halo_s,
    halo_r,
    th_s,
    th_r,
    e_s,
    e_r,
    dz_s,
    dz_r,
    dx_s,
    dx_r,
    p1_s,
    p1_r,
    l_s,
    l_r,
    l1_s,
    r2_s,
    r3_s,
    r_s,
    up_s,
    x_s,
    x_r,
    sib_s,
    sib_r,
):
    g = lax.axis_index("group")
    core = lax.rem(g, 2)
    z = lax.rem(g // 2, NZ)
    x = g // (2 * NZ)
    ngroups = 2 * NZ * NX

    def at(xx, zz, cc):
        return (xx * NZ + zz) * 2 + cc

    sib = at(x, z, 1 - core)
    gnext = lax.rem(g + 1, ngroups)
    gprev = lax.rem(g + ngroups - 1, ngroups)

    def zpeer(d):
        return lax.rem(z + d, NZ)

    def xpeer(d):
        return lax.rem(x + d, NX)

    barrier = pltpu.get_barrier_semaphore()

    def hello(peer):
        pl.semaphore_signal(barrier, inc=1, device_id={"group": peer}, device_id_type=MESH)

    for d in range(1, NZ):
        hello(at(x, zpeer(d), core))
    for d in range(1, NX):
        hello(at(xpeer(d), z, core))
    for peer in (sib, gnext, gprev):
        hello(peer)
    n_hello = NZ - 1 + NX - 1 + 3

    in_copies = [
        pltpu.make_async_copy(mixed_h, mixed, in_s.at[0]),
        pltpu.make_async_copy(lam_h, lam, in_s.at[1]),
        pltpu.make_async_copy(gate_h, gate, in_s.at[2]),
    ]
    for cp in in_copies:
        cp.start()

    def rcopy(src, dst, ss, rs, peer):
        return pltpu.make_async_remote_copy(
            src_ref=src,
            dst_ref=dst,
            send_sem=ss,
            recv_sem=rs,
            device_id={"group": peer},
            device_id_type=MESH,
        )

    first = g * TOK
    b1 = segl[0]
    b2 = segl[0] + segl[1]

    def seg_of(pos):
        s = (pos >= b1).astype(jnp.int32) + (pos >= b2).astype(jnp.int32)
        return jnp.where(pos >= 0, s, -1)

    lane_pos = first + lax.broadcasted_iota(jnp.int32, (8, TOK), 1)[0:1]
    seg_row = seg_of(lane_pos)
    last_row = seg_of(jnp.full((1, TOK), first + TOK - 1, jnp.int32))
    prev_row = seg_of(jnp.full((1, TOK), first - 1, jnp.int32))

    c = ld[...]
    lane = lax.broadcasted_iota(jnp.int32, (HEADS, TOK), 1)
    step = 1
    while step < TOK:
        c = c + jnp.where(lane >= step, pltpu.roll(c, step, 1), 0.0)
        step *= 2
    cum[...] = c
    c_end = c[:, TOK - 1 : TOK]
    endw[...] = jnp.exp(c_end - c) * (seg_row == last_row).astype(F32)
    entry[...] = jnp.exp(c) * (seg_row == prev_row).astype(F32)
    theta[0] = jnp.broadcast_to(jnp.exp(c_end), (HEADS, 128)) * (last_row == prev_row).astype(F32)[
        :, 0:128
    ]
    cpad = jnp.concatenate([c, jnp.zeros((128 - HEADS, TOK), F32)], axis=0)
    cumt[...] = jnp.concatenate([cpad[:, 0:128].T, cpad[:, 128:256].T], axis=0)

    si = lax.broadcasted_iota(jnp.int32, (128, 128), 0)
    ti = lax.broadcasted_iota(jnp.int32, (128, 128), 1)
    diff = si ^ ti
    lv = jnp.zeros((128, 128), jnp.int32)
    for b in range(7):
        lv = lv + (diff >= 2**b).astype(jnp.int32)
    lev[...] = lv

    col_pos = first + lax.broadcasted_iota(jnp.int32, (TOK, 256), 0)
    seg_col = seg_of(col_pos)
    same = [None] + [seg_of(col_pos - t) == seg_col for t in range(1, TAPS)]

    def taps(cols, rows, cur):
        total = cb[cols].reshape(1, BR) + cw[0:1, cols] * cur
        for t in range(1, TAPS):
            piece = pad[8 - t : 8 - t + rows, :]
            total = total + cw[t : t + 1, cols] * jnp.where(same[t][0:rows], piece, 0.0)
        return total * (1.0 / (1.0 + jnp.exp(-total)))

    pad[0:8, :] = jnp.zeros((8, BR), F32)

    def conv_rows(i, _):
        cols = pl.ds(pl.multiple_of(i * BR, BR), BR)
        cur = mixed[:, cols].astype(F32)
        pad[8 : 8 + TOK, :] = cur
        act[:, cols] = taps(cols, TOK, cur)
        return 0

    def conv_first(i, _):
        cols = pl.ds(pl.multiple_of(i * BR, BR), BR)
        cur = mixed[0:16, cols].astype(F32)[0:8]
        pad[8:16, :] = cur
        pad[0:8, :] = halo[:, cols].astype(F32)[8:16]
        act[0:8, cols] = taps(cols, 8, cur)
        return 0

    in_copies[0].wait()
    lax.fori_loop(0, CONV_A, conv_rows, 0)
    pl.semaphore_wait(barrier, n_hello)

    halo_copy = rcopy(mixed.at[pl.ds(TOK - HALO, HALO)], halo, halo_s, halo_r, gnext)
    halo_copy.start()
    th_copy = rcopy(theta.at[0], theta.at[1], th_s, th_r, sib)
    th_copy.start()
    lax.fori_loop(CONV_A, CH // BR, conv_rows, 0)

    th_copy.wait_recv()
    dtab[z] = theta[0] * theta[1]

    def dz_copy(to, frm):
        return rcopy(dtab.at[frm], dtab.at[frm], dz_s.at[to], dz_r.at[frm], at(x, to, core))

    def dx_copy(to, frm):
        return rcopy(dline.at[frm], dline.at[frm], dx_s.at[to], dx_r.at[frm], at(to, z, core))

    def over_z(f):
        def go(d, _):
            f(zpeer(d))
            return 0

        lax.fori_loop(1, NZ, go, 0)

    def over_x(f):
        def go(d, _):
            f(xpeer(d))
            return 0

        lax.fori_loop(1, NX, go, 0)

    over_z(lambda o: dz_copy(o, z).start())

    halo_copy.wait_recv()
    lax.fori_loop(0, CH // BR, conv_first, 0)
    keys[...] = act[:, WIDTH : WIDTH + STATE].astype(BF16)
    quer[...] = act[:, WIDTH + STATE : CH].astype(BF16)

    def turn(i, _):
        base = pl.multiple_of(i * BR, BR)
        xst[pl.ds(base, BR), :] = act[:, pl.ds(base, BR)].T.astype(BF16)
        return 0

    lax.fori_loop(0, NB, turn, 0)

    def e_copy(i):
        rows = pl.ds(pl.multiple_of(i * PB, PB), PB)
        return rcopy(ef.at[rows], sibe.at[rows], e_s.at[i], e_r.at[i], sib)

    def e_block(which, n):
        return which * (NPB // 2) + lax.rem(n + z // 2 + 2, NPB // 2)

    def e_step(i):
        base = pl.multiple_of(i * PB, PB)
        parts = []
        for j in range(NSG):
            w = endw[pl.ds(i * NSG + j, 1), :]
            xt = xst[pl.ds(pl.multiple_of(base + j * HD, HD), HD), :]
            parts.append((xt.astype(F32) * w).astype(BF16))
        e = jnp.dot(jnp.concatenate(parts, axis=0), keys[...], preferred_element_type=F32)
        ef[pl.ds(base, PB), :] = e
        e_copy(i).start()

    def e_other(n, _):
        e_step(e_block(1 - core, n))
        return 0

    lax.fori_loop(0, NPB // 2, e_other, 0)

    xrow = lax.broadcasted_iota(jnp.int32, (16, 128), 0) // 3

    def encode(blocks):
        q = []
        ex = jnp.zeros((16, 128), F32)
        for k in range(NSG):
            top = jnp.max(jnp.abs(blocks[k]), axis=0, keepdims=True)
            e = jnp.ceil(jnp.log2(jnp.maximum(top, 1e-30))) - 14.0
            q.append(jnp.floor(blocks[k] * (1.0 / jnp.exp2(e)) + 0.5))
            ex = jnp.where(xrow == k, e, ex)
        return jnp.concatenate(q + [ex], axis=0).astype(jnp.int32).astype(jnp.int16)

    def decode(ref):
        ex = jnp.exp2(ref[PR:XP, :].astype(jnp.int32).astype(F32))
        return [
            ref[k * SG : (k + 1) * SG, :].astype(jnp.int32).astype(F32) * ex[3 * k : 3 * k + 1]
            for k in range(NSG)
        ]

    def head_of(o, k):
        return core * (HEADS // 2) + (o * NSG + k) // 2

    def p1_copy(to, frm):
        return rcopy(p1s.at[to], p1r.at[frm], p1_s.at[to], p1_r.at[frm], at(x, to, core))

    def chip_step(o):
        blocks = []
        for k in range(NSG):
            rows = pl.ds(pl.multiple_of(core * HALF + o * PR + k * SG, SG), SG)
            own, other = ef[rows, :], sibe[rows, :]
            h = pl.ds(head_of(o, k), 1)
            low = jnp.where(core == 0, own, other)
            high = jnp.where(core == 0, other, own)
            d = jnp.where(core == 0, theta[1, h, :], theta[0, h, :])
            blocks.append(low * d + high)
        p1s[o] = encode(blocks)

        @pl.when(o != z)
        def _():
            p1_copy(o, z).start()

        @pl.when(o == z)
        def _():
            p1r[o] = p1s[o]

    def e_mine(n, _):
        i = e_block(core, n)
        e_step(i)
        e_copy(i).wait_recv()
        for m in range(2):
            chip_step(2 * lax.rem(n + z // 2 + 2, NPB // 2) + m)
        return 0

    lax.fori_loop(0, NPB // 2, e_mine, 0)

    over_z(lambda o: dz_copy(o, o).wait_recv())
    pair = [dtab[2 * j] * dtab[2 * j + 1] for j in range(NZ // 2)]
    quad = [pair[0] * pair[1], pair[2] * pair[3]]
    dline[x] = quad[0] * quad[1]
    over_x(lambda o: dx_copy(o, x).start())


    me = core * NZ + z

    def l_copy(lvl, src, o, frm):
        return rcopy(
            src, lbuf.at[lvl, core * NZ + frm], l_s.at[lvl, o], l_r.at[lvl, frm], at(x, o, core)
        )

    def l1_copy(o):
        return rcopy(
            p1s.at[o],
            lbuf.at[0, core * NZ + o],
            l1_s.at[o],
            l_r.at[0, o],
            at(x, zpeer(1), core),
        )

    def l1_direct(do):
        for d in range(4):
            do(l1_copy(zpeer(NZ - d)))


    s_t = lax.dot_general(
        keys[...], quer[...], (((1,), (1,)), ((), ())), preferred_element_type=F32
    )
    rowi = lax.broadcasted_iota(jnp.int32, (TOK, TOK), 0)
    coli = lax.broadcasted_iota(jnp.int32, (TOK, TOK), 1)
    ok = (rowi <= coli) & (seg_col == seg_row)
    sct[...] = jnp.where(ok, s_t, 0.0)

    def local_heads(i, _):
        rolled = pltpu.roll(cumt[...], lax.rem(128 - i * HPB, 128), 1)
        for j in range(HPB):
            h = i * HPB + j
            rows = pl.ds(pl.multiple_of(h * HD, HD), HD)
            ccol = rolled[:, j : j + 1]
            crow = cum[pl.ds(h, 1), :]

            def lam_row(l, lo):
                return lam[l, pl.ds(h, 1), :][:, lo : lo + 128]

            def picked(lo):
                p = jnp.broadcast_to(lam_row(7, lo), (128, 128))
                for l in range(7):
                    p = jnp.where(lev[...] == l, lam_row(l, lo), p)
                return p

            def mix(slo, tlo, pick):
                gap = crow[:, tlo : tlo + 128] - ccol[slo : slo + 128]
                decay = jnp.exp(jnp.minimum(gap, 0.0))
                return (sct[slo : slo + 128, tlo : tlo + 128] * pick * decay).astype(BF16)

            m00 = mix(0, 0, picked(0))
            m01 = mix(0, 128, lam_row(8, 128))
            m11 = mix(128, 128, picked(128))
            xs = xst[rows, :]
            left = jnp.dot(xs[:, 0:128], m00, preferred_element_type=F32)
            right = jnp.dot(xs, jnp.concatenate([m01, m11], axis=0), preferred_element_type=F32)
            acc[rows, :] = jnp.concatenate([left, right], axis=1) + skip[h] * xs.astype(F32)
        return 0

    pair = [dtab[2 * j] * dtab[2 * j + 1] for j in range(NZ // 2)]
    quad = [pair[0] * pair[1], pair[2] * pair[3]]
    one = jnp.ones((HEADS, 128), F32)
    pbuf[1] = jnp.where(core == 1, theta[1], one)
    below = jnp.where(lax.rem(z, 2) == 1, dtab[jnp.maximum(z - 1, 0)], one)
    pbuf[2] = pbuf[1] * below
    pbuf[3] = pbuf[2] * jnp.where(
        lax.rem(z // 2, 2) == 1, jnp.where(z >= 4, pair[2], pair[0]), one
    )
    pbuf[4] = pbuf[3] * jnp.where(z >= 4, quad[0], one)

    in_copies[1].wait()
    lax.fori_loop(0, LOCAL_A, local_heads, 0)

    over_z(lambda o: p1_copy(o, o).wait_recv())
    cs = [decode(p1r.at[j]) for j in range(NZ)]
    b01, b45, b03, b07 = [], [], [], []
    for k in range(NSG):
        h = pl.ds(head_of(z, k), 1)
        d = [dtab[j, h, :] for j in range(NZ)]
        pr = [cs[2 * j][k] * d[2 * j + 1] + cs[2 * j + 1][k] for j in range(NZ // 2)]
        lo = pr[0] * (d[2] * d[3]) + pr[1]
        hi = pr[2] * (d[6] * d[7]) + pr[3]
        b01.append(pr[0])
        b45.append(pr[2])
        b03.append(lo)
        b07.append(lo * (d[4] * d[5] * d[6] * d[7]) + hi)
    osnd[3] = encode(b07)

    def x_copy(to, frm):
        return rcopy(osnd.at[3], tr.at[frm], x_s.at[to], x_r.at[frm], at(to, z, core))

    def x_to(o):
        return (o > x) & ((o < 3) | (x == 2))

    def send_x(o):
        @pl.when(x_to(o))
        def _():
            x_copy(o, x).start()

    over_x(send_x)
    osnd[2] = encode(b03)
    osnd[0] = encode(b01)
    osnd[1] = encode(b45)

    def sib_copy(lvl, o):
        dst = lbuf.at[lvl, core * NZ + o]
        return rcopy(dst, dst, sib_s.at[lvl, o], sib_r.at[lvl, o], sib)

    def sib_wait(lvl, o):
        dst = lbuf.at[lvl, (1 - core) * NZ + o]
        rcopy(dst, dst, sib_s.at[lvl, o], sib_r.at[lvl, o], sib).wait_recv()

    def bit(v, b):
        return lax.rem(v // 2**b, 2) == 1

    def keep(lvl, src):
        lbuf[lvl, me] = src
        sib_copy(lvl, z).start()

    def mir(o):
        return jnp.where(z >= 6, lax.rem(11 - o, NZ), o)

    l3_to = jnp.where(z >= 2, 4, 7)
    l3_end = (z == 4) | (z == 7)
    l3_mid = (z == 5) | (z == 6)

    def l3_own(do):
        @pl.when(z < 4)
        def _():
            do(lambda: l_copy(2, osnd.at[2], l3_to, z))

        @pl.when(z >= 4)
        def _():
            do(lambda: l_copy(2, osnd.at[2], jnp.where(l3_end, mir(5), mir(4)), z))
            do(lambda: l_copy(2, osnd.at[2], mir(6), z))

    def l3_on(slot, o, to):
        dst = lbuf.at[2, core * NZ + o]
        return rcopy(dst, dst, r3_s.at[slot, o], l_r.at[2, o], at(x, to, core))

    def l3_in(o):
        l_copy(2, lbuf.at[2, me], o, o).wait_recv()

    def l3_first():
        @pl.when(l3_end)
        def _():
            for q in (3, 2):
                o = mir(q)
                l3_in(o)
                l3_on(0, o, mir(5)).start()
                l3_on(1, o, mir(6)).start()
                sib_copy(2, o).start()

    def l3_rest():
        @pl.when(l3_mid)
        def _():
            for q in (6, 7, 0, 1):
                o = mir(q)
                l3_in(o)
                l3_on(0, o, mir(4)).start()
                sib_copy(2, o).start()
            for q in (4, 3, 2):
                o = mir(q)
                l3_in(o)
                sib_copy(2, o).start()

        @pl.when(l3_end)
        def _():
            for q in (5, 6, 7, 0, 1):
                o = mir(q)
                l3_in(o)
                sib_copy(2, o).start()

    def l3_on_done():
        @pl.when(l3_end)
        def _():
            for q in (3, 2):
                l3_on(0, mir(q), mir(5)).wait_send()
                l3_on(1, mir(q), mir(6)).wait_send()

        @pl.when(l3_mid)
        def _():
            for q in (6, 7, 0, 1):
                l3_on(0, mir(q), mir(4)).wait_send()

    def l2_own(do):
        for p in (2, 6):
            r = lax.rem(z + NZ - p, NZ)
            to = jnp.where((r == 1) | (r >= 5), p, p + 1)
            do(lambda to=to, p=p: l_copy(1, osnd.at[p // 4], to, z))

    l2_other = jnp.where(lax.rem(z, 2) == 0, z + 1, z - 1)

    def l2_off(d):
        return lax.rem(jnp.where(lax.rem(z, 2) == 0, z + NZ - d, z + d), NZ)

    def l2_on(o):
        dst = lbuf.at[1, core * NZ + o]
        return rcopy(dst, dst, r2_s.at[o], l_r.at[1, o], at(x, l2_other, core))

    def l2_in(o):
        l_copy(1, lbuf.at[1, me], o, o).wait_recv()

    def l2_first():
        @pl.when(bit(z, 1))
        def _():
            for d in (1, 2, 3):
                l2_in(l2_off(d))
                l2_on(l2_off(d)).start()
                sib_copy(1, l2_off(d)).start()

    def l2_rest():
        @pl.when(bit(z, 1))
        def _():
            for d in (7, 6, 5, 4):
                l2_in(l2_off(d))
                sib_copy(1, l2_off(d)).start()

    l3_own(lambda c: c().start())
    l2_own(lambda c: c().start())

    def l1_owner(do):
        for d in (1, 2, 3):
            to = zpeer(NZ - d)

            @pl.when(lax.rem(to, 2) == 1)
            def _(to=to):
                do(
                    lambda: l_copy(
                        0, p1r.at[lax.rem(to + NZ - 1, NZ)], to, z
                    )
                )

    @pl.when(lax.rem(z, 2) == 0)
    def _():
        l1_direct(lambda c: c.start())

    l1_owner(lambda c: c().start())

    @pl.when(lax.rem(z, 2) == 1)
    def _():
        keep(0, p1r[jnp.maximum(z - 1, 0)])

    @pl.when(z >= 4)
    def _():
        keep(2, osnd[2])

    @pl.when(bit(z, 1))
    def _():
        keep(1, osnd[z // 4])

    def sib_all(lvl):
        def go(o, _):
            sib_wait(lvl, o)
            return 0

        lax.fori_loop(0, NZ, go, 0)

    def far(level):
        def body(i, _):
            base = pl.multiple_of(i * PB, PB)
            if level == 0:
                state = sibe[pl.ds(base, PB), :].astype(BF16)
            else:
                parts = []
                for m in range(2):
                    v = decode(lbuf.at[level - 1, 2 * i + m])
                    for k in range(NSG):
                        p = pbuf[level, pl.ds(i * NSG + (m * NSG + k) // 2, 1), :]
                        parts.append((v[k] * p).astype(BF16))
                state = jnp.concatenate(parts, axis=0)
            read = lax.dot_general(
                state, quer[...], (((1,), (1,)), ((), ())), preferred_element_type=F32
            )
            for j in range(NSG):
                h = pl.ds(i * NSG + j, 1)
                coef = lam[9 + level, h, :] * entry[h, :]
                rows = pl.ds(pl.multiple_of(base + j * HD, HD), HD)
                acc[rows, :] = acc[rows, :] + read[j * HD : (j + 1) * HD] * coef
            return 0

        lax.fori_loop(0, NPB, body, 0)

    def gate_block(i, _):
        cols = pl.ds(pl.multiple_of(i * BR, BR), BR)
        v = gate[:, cols].astype(F32)
        gt[cols, :] = (v * (1.0 / (1.0 + jnp.exp(-v)))).T
        return 0

    lax.fori_loop(LOCAL_A, NB, local_heads, 0)
    in_copies[2].wait()
    lax.fori_loop(0, NB, gate_block, 0)

    def wait_e2(n, _):
        e_copy((1 - core) * (NPB // 2) + n).wait_recv()
        return 0

    lax.fori_loop(0, NPB // 2, wait_e2, 0)

    @pl.when(core == 1)
    def _():
        far(0)

    over_x(lambda o: dx_copy(o, o).wait_recv())
    pbuf[5] = pbuf[4] * jnp.where(lax.rem(x, 2) == 1, dline[jnp.maximum(x - 1, 0)], one)

    def x_in(frm):
        x_copy(frm, frm).wait_recv()

    NEAR = (2, 6, 1, 7)

    def spread(lvl, src):
        for d in NEAR:
            l_copy(lvl, src, zpeer(d), z).start()

    def r_copy(lvl, d, frm):
        dst = lbuf.at[lvl, core * NZ + frm]
        to = zpeer(d)
        return rcopy(dst, dst, r_s.at[to], l_r.at[lvl, frm], at(x, to, core))

    def up_copy(src, frm):
        return rcopy(
            src, lbuf.at[4, core * NZ + frm], up_s.at[frm], l_r.at[4, frm], at(xpeer(1), z, core)
        )

    def gather(lvl, up):
        def arrived(frm):
            l_copy(lvl, lbuf.at[lvl, me], frm, frm).wait_recv()

        def hand_on(frm):
            sib_copy(lvl, frm).start()
            if up:
                up_copy(lbuf.at[lvl, core * NZ + frm], frm).start()

        def pull(d):
            arrived(zpeer(d))
            hand_on(zpeer(d))

        arrived(zpeer(6))
        r_copy(lvl, 1, zpeer(6)).start()

        hand_on(zpeer(6))
        arrived(zpeer(2))
        r_copy(lvl, 7, zpeer(2)).start()
        r_copy(lvl, 6, zpeer(2)).start()

        hand_on(zpeer(2))
        for d in (1, 7, 3, 5, 4):
            pull(d)

    def send_l4(frm):
        spread(3, tr.at[frm])
        keep(3, tr[frm])

    def send_l5():
        t0, t1 = decode(tr.at[0]), decode(tr.at[1])
        osnd[4] = encode(
            [t0[k] * dline[1, pl.ds(head_of(z, k), 1), :] + t1[k] for k in range(NSG)]
        )
        spread(4, osnd.at[4])
        up_copy(osnd.at[4], z).start()
        keep(4, osnd[4])

    @pl.when(x == 1)
    def _():
        x_in(0)
        send_l4(0)

    @pl.when(x == 3)
    def _():
        x_in(2)
        send_l4(2)

    @pl.when(x == 2)
    def _():
        x_in(1)
        x_in(0)
        send_l5()

    l3_first()
    l2_first()

    @pl.when(lax.rem(x, 2) == 1)
    def _():
        gather(3, False)

    @pl.when(x == 2)
    def _():
        gather(4, True)

    @pl.when(lax.rem(z, 2) == 1)
    def _():
        def go(o):
            l_copy(0, lbuf.at[0, me], o, o).wait_recv()
            sib_copy(0, o).start()

        over_z(go)

    l3_rest()
    l2_rest()

    @pl.when(lax.rem(z, 2) == 1)
    def _():
        sib_all(0)
        far(1)

    @pl.when(bit(z, 1))
    def _():
        sib_all(1)
        far(2)

    @pl.when(z >= 4)
    def _():
        sib_all(2)
        far(3)

    @pl.when(x == 3)
    def _():
        def go(o, _):
            up_copy(osnd.at[4], o).wait_recv()
            sib_copy(4, o).start()
            return 0

        lax.fori_loop(0, NZ, go, 0)

    @pl.when(lax.rem(x, 2) == 1)
    def _():
        sib_all(3)
        far(4)

    @pl.when(x >= 2)
    def _():
        sib_all(4)
        far(5)

    def gate_step(i, ssq):
        rows = pl.ds(pl.multiple_of(i * BR, BR), BR)
        v = acc[rows, :] * gt[rows, :]
        acc[rows, :] = v
        return ssq + jnp.sum((v * v).reshape(BR // 8, 8, TOK), axis=0)

    ssq = lax.fori_loop(0, NB, gate_step, jnp.zeros((8, TOK), F32))
    scale = lax.rsqrt(jnp.sum(ssq, axis=0, keepdims=True) * (1.0 / WIDTH) + EPS)

    def out_step(i, _):
        cols = pl.ds(pl.multiple_of(i * BR, BR), BR)
        v = (acc[cols, :] * scale).T
        out[:, cols] = (v * ng[cols].reshape(1, BR)).astype(BF16)
        return 0

    lax.fori_loop(0, NB, out_step, 0)

    halo_copy.wait_send()
    th_copy.wait_send()

    def e_done(i, _):
        e_copy(i).wait_send()
        return 0

    lax.fori_loop(0, NPB, e_done, 0)
    over_z(lambda o: dz_copy(o, z).wait_send())
    over_z(lambda o: p1_copy(o, z).wait_send())
    over_x(lambda o: dx_copy(o, x).wait_send())

    def x_done(o):
        @pl.when(x_to(o))
        def _():
            x_copy(o, x).wait_send()

    over_x(x_done)

    l3_own(lambda c: c().wait_send())
    l3_on_done()
    l2_own(lambda c: c().wait_send())

    @pl.when(bit(z, 1))
    def _():
        for d in (1, 2, 3):
            l2_on(l2_off(d)).wait_send()

    def spread_done(lvl):
        for d in NEAR:
            l_copy(lvl, osnd.at[4], zpeer(d), z).wait_send()
        for d in (1, 7, 6):
            r_copy(lvl, d, z).wait_send()

    pl.when(lax.rem(x, 2) == 1)(lambda: spread_done(3))

    @pl.when(x == 2)
    def _():
        spread_done(4)

        def go(o, _):
            up_copy(osnd.at[4], o).wait_send()
            return 0

        lax.fori_loop(0, NZ, go, 0)

    def sib_done(lvl):
        def go(o, _):
            sib_copy(lvl, o).wait_send()
            return 0

        lax.fori_loop(0, NZ, go, 0)

    @pl.when(lax.rem(z, 2) == 0)
    def _():
        l1_direct(lambda c: c.wait_send())

    l1_owner(lambda c: c().wait_send())
    pl.when(lax.rem(z, 2) == 1)(lambda: sib_done(0))
    pl.when(bit(z, 1))(lambda: sib_done(1))
    pl.when(z >= 4)(lambda: sib_done(2))
    pl.when(lax.rem(x, 2) == 1)(lambda: sib_done(3))
    pl.when(x >= 2)(lambda: sib_done(4))


def per_device(
    mixed_input,
    conv_weight,
    conv_bias,
    gate_input,
    log_decay,
    level_weights,
    skip_gain,
    norm_gain,
    seg_lengths,
):
    vmem = pl.BlockSpec(memory_space=pltpu.VMEM)
    hbm = pl.BlockSpec(memory_space=pl.ANY)
    smem = pl.BlockSpec(memory_space=pltpu.SMEM)
    dma = pltpu.SemaphoreType.DMA
    return pl.pallas_call(
        kernel,
        out_shape=pltpu.VMEM((TOK, WIDTH), BF16),
        in_specs=[hbm, hbm, vmem, hbm] + [vmem] * 3 + [smem] * 2,
        out_specs=vmem,
        scratch_shapes=[
            pltpu.VMEM((TOK, CH), BF16),
            pltpu.VMEM((TOK, WIDTH), BF16),
            pltpu.VMEM((20, HEADS, TOK), F32),
            pltpu.VMEM((HALO, CH), BF16),
            pltpu.VMEM((TOK + 8, BR), F32),
            pltpu.VMEM((TOK, CH), F32),
            pltpu.VMEM((WIDTH, TOK), BF16),
            pltpu.VMEM((TOK, STATE), BF16),
            pltpu.VMEM((TOK, STATE), BF16),
            pltpu.VMEM((WIDTH, STATE), F32),
            pltpu.VMEM((WIDTH, STATE), F32),
            pltpu.VMEM((NZ, XP, STATE), jnp.int16),
            pltpu.VMEM((NZ, XP, STATE), jnp.int16),
            pltpu.VMEM((5, XP, STATE), jnp.int16),
            pltpu.VMEM((NX, XP, STATE), jnp.int16),
            pltpu.VMEM((5, 2 * NZ, XP, STATE), jnp.int16),
            pltpu.VMEM((NZ, HEADS, 128), F32),
            pltpu.VMEM((NX, HEADS, 128), F32),
            pltpu.VMEM((2, HEADS, 128), F32),
            pltpu.VMEM((6, HEADS, 128), F32),
            pltpu.VMEM((HEADS, TOK), F32),
            pltpu.VMEM((TOK, 128), F32),
            pltpu.VMEM((HEADS, TOK), F32),
            pltpu.VMEM((HEADS, TOK), F32),
            pltpu.VMEM((TOK, TOK), F32),
            pltpu.VMEM((128, 128), jnp.int32),
            pltpu.VMEM((WIDTH, TOK), F32),
            pltpu.VMEM((WIDTH, TOK), F32),
            dma((3,)),
            dma,
            dma,
            dma,
            dma,
            dma((NPB,)),
            dma((NPB,)),
            dma((NZ,)),
            dma((NZ,)),
            dma((NX,)),
            dma((NX,)),
            dma((NZ,)),
            dma((NZ,)),
            dma((5, NZ)),
            dma((5, NZ)),
            dma((NZ,)),
            dma((NZ,)),
            dma((2, NZ)),
            dma((NZ,)),
            dma((NZ,)),
            dma((NX,)),
            dma((NX,)),
            dma((5, NZ)),
            dma((5, NZ)),
        ],
        compiler_params=pltpu.CompilerParams(
            collective_id=0, has_side_effects=True, vmem_limit_bytes=60 * 1024 * 1024
        ),
        name="layer",
    )(
        mixed_input,
        gate_input,
        log_decay,
        jnp.transpose(level_weights, (1, 0, 2)),
        conv_weight,
        conv_bias,
        norm_gain,
        skip_gain,
        seg_lengths,
    )


def solution(mesh):
    in_specs = (
        P(("batch", "group"), None),
        P(),
        P(),
        P(("batch", "group"), None),
        P(None, ("batch", "group")),
        P(None, None, ("batch", "group")),
        P(),
        P(),
        P("batch"),
    )
    out_specs = P(("batch", "group"), None)
    return jax.shard_map(
        per_device, mesh=mesh, in_specs=in_specs, out_specs=out_specs, check_vma=False
    )
```

```python
import jax
import jax.numpy as jnp
from jax import lax
from jax.experimental import pallas as pl
from jax.experimental.pallas import tpu as pltpu
from jax.sharding import PartitionSpec as P

EPS = 1e-05
F32 = jnp.float32
BF16 = jnp.bfloat16
MESH = pl.DeviceIdType.MESH

TOK = 256
WIDTH = 2560
HEADS = 40
HD = 64
STATE = 128
CH = 2816
TAPS = 4
NX, NZ = 4, 8
HALF = WIDTH // 2
HALO = 16
PR = HALF // NZ
SG = 32
NSG = PR // SG
XP = PR + 16
PB = 2 * PR
NPB = WIDTH // PB
BR = 256
NB = WIDTH // BR
HPB = BR // HD
LOCAL_A = 8
CONV_A = 4


def kernel(
    mixed_h,
    gate_h,
    ld,
    lam_h,
    cw,
    cb,
    ng,
    skip,
    segl,
    out,
    mixed,
    gate,
    lam,
    halo,
    pad,
    act,
    xst,
    keys,
    quer,
    ef,
    sibe,
    p1s,
    p1r,
    osnd,
    tr,
    lbuf,
    dtab,
    dline,
    theta,
    pbuf,
    cum,
    cumt,
    endw,
    entry,
    sct,
    lev,
    acc,
    gt,
    in_s,
    halo_s,
    halo_r,
    th_s,
    th_r,
    e_s,
    e_r,
    dz_s,
    dz_r,
    dx_s,
    dx_r,
    p1_s,
    p1_r,
    l_s,
    l_r,
    l1_s,
    r2_s,
    r3_s,
    r_s,
    up_s,
    x_s,
    x_r,
    sib_s,
    sib_r,
):
    g = lax.axis_index("group")
    core = lax.rem(g, 2)
    z = lax.rem(g // 2, NZ)
    x = g // (2 * NZ)
    ngroups = 2 * NZ * NX

    def at(xx, zz, cc):
        return (xx * NZ + zz) * 2 + cc

    sib = at(x, z, 1 - core)
    gnext = lax.rem(g + 1, ngroups)
    gprev = lax.rem(g + ngroups - 1, ngroups)

    def zpeer(d):
        return lax.rem(z + d, NZ)

    def xpeer(d):
        return lax.rem(x + d, NX)

    barrier = pltpu.get_barrier_semaphore()

    def hello(peer):
        pl.semaphore_signal(barrier, inc=1, device_id={"group": peer}, device_id_type=MESH)

    for d in range(1, NZ):
        hello(at(x, zpeer(d), core))
    for d in range(1, NX):
        hello(at(xpeer(d), z, core))
    for peer in (sib, gnext, gprev):
        hello(peer)
    n_hello = NZ - 1 + NX - 1 + 3

    in_copies = [
        pltpu.make_async_copy(mixed_h, mixed, in_s.at[0]),
        pltpu.make_async_copy(lam_h, lam, in_s.at[1]),
        pltpu.make_async_copy(gate_h, gate, in_s.at[2]),
    ]
    for cp in in_copies:
        cp.start()

    def rcopy(src, dst, ss, rs, peer):
        return pltpu.make_async_remote_copy(
            src_ref=src,
            dst_ref=dst,
            send_sem=ss,
            recv_sem=rs,
            device_id={"group": peer},
            device_id_type=MESH,
        )

    first = g * TOK
    b1 = segl[0]
    b2 = segl[0] + segl[1]

    def seg_of(pos):
        s = (pos >= b1).astype(jnp.int32) + (pos >= b2).astype(jnp.int32)
        return jnp.where(pos >= 0, s, -1)

    lane_pos = first + lax.broadcasted_iota(jnp.int32, (8, TOK), 1)[0:1]
    seg_row = seg_of(lane_pos)
    last_row = seg_of(jnp.full((1, TOK), first + TOK - 1, jnp.int32))
    prev_row = seg_of(jnp.full((1, TOK), first - 1, jnp.int32))

    c = ld[...]
    lane = lax.broadcasted_iota(jnp.int32, (HEADS, TOK), 1)
    step = 1
    while step < TOK:
        c = c + jnp.where(lane >= step, pltpu.roll(c, step, 1), 0.0)
        step *= 2
    cum[...] = c
    c_end = c[:, TOK - 1 : TOK]
    endw[...] = jnp.exp(c_end - c) * (seg_row == last_row).astype(F32)
    entry[...] = jnp.exp(c) * (seg_row == prev_row).astype(F32)
    theta[0] = jnp.broadcast_to(jnp.exp(c_end), (HEADS, 128)) * (last_row == prev_row).astype(F32)[
        :, 0:128
    ]
    cpad = jnp.concatenate([c, jnp.zeros((128 - HEADS, TOK), F32)], axis=0)
    cumt[...] = jnp.concatenate([cpad[:, 0:128].T, cpad[:, 128:256].T], axis=0)

    si = lax.broadcasted_iota(jnp.int32, (128, 128), 0)
    ti = lax.broadcasted_iota(jnp.int32, (128, 128), 1)
    diff = si ^ ti
    lv = jnp.zeros((128, 128), jnp.int32)
    for b in range(7):
        lv = lv + (diff >= 2**b).astype(jnp.int32)
    lev[...] = lv

    col_pos = first + lax.broadcasted_iota(jnp.int32, (TOK, 256), 0)
    seg_col = seg_of(col_pos)
    same = [None] + [seg_of(col_pos - t) == seg_col for t in range(1, TAPS)]

    def taps(cols, rows, cur):
        total = cb[cols].reshape(1, BR) + cw[0:1, cols] * cur
        for t in range(1, TAPS):
            piece = pad[8 - t : 8 - t + rows, :]
            total = total + cw[t : t + 1, cols] * jnp.where(same[t][0:rows], piece, 0.0)
        return total * (1.0 / (1.0 + jnp.exp(-total)))

    pad[0:8, :] = jnp.zeros((8, BR), F32)

    def conv_rows(i, _):
        cols = pl.ds(pl.multiple_of(i * BR, BR), BR)
        cur = mixed[:, cols].astype(F32)
        pad[8 : 8 + TOK, :] = cur
        act[:, cols] = taps(cols, TOK, cur)
        return 0

    def conv_first(i, _):
        cols = pl.ds(pl.multiple_of(i * BR, BR), BR)
        cur = mixed[0:16, cols].astype(F32)[0:8]
        pad[8:16, :] = cur
        pad[0:8, :] = halo[:, cols].astype(F32)[8:16]
        act[0:8, cols] = taps(cols, 8, cur)
        return 0

    in_copies[0].wait()
    lax.fori_loop(0, CONV_A, conv_rows, 0)
    pl.semaphore_wait(barrier, n_hello)

    halo_copy = rcopy(mixed.at[pl.ds(TOK - HALO, HALO)], halo, halo_s, halo_r, gnext)
    halo_copy.start()
    th_copy = rcopy(theta.at[0], theta.at[1], th_s, th_r, sib)
    th_copy.start()
    lax.fori_loop(CONV_A, CH // BR, conv_rows, 0)

    th_copy.wait_recv()
    dtab[z] = theta[0] * theta[1]

    def dz_copy(to, frm):
        return rcopy(dtab.at[frm], dtab.at[frm], dz_s.at[to], dz_r.at[frm], at(x, to, core))

    def dx_copy(to, frm):
        return rcopy(dline.at[frm], dline.at[frm], dx_s.at[to], dx_r.at[frm], at(to, z, core))

    def over_z(f):
        def go(d, _):
            f(zpeer(d))
            return 0

        lax.fori_loop(1, NZ, go, 0)

    def over_x(f):
        def go(d, _):
            f(xpeer(d))
            return 0

        lax.fori_loop(1, NX, go, 0)

    over_z(lambda o: dz_copy(o, z).start())

    halo_copy.wait_recv()
    lax.fori_loop(0, CH // BR, conv_first, 0)
    keys[...] = act[:, WIDTH : WIDTH + STATE].astype(BF16)
    quer[...] = act[:, WIDTH + STATE : CH].astype(BF16)

    def turn(i, _):
        base = pl.multiple_of(i * BR, BR)
        xst[pl.ds(base, BR), :] = act[:, pl.ds(base, BR)].T.astype(BF16)
        return 0

    lax.fori_loop(0, NB, turn, 0)

    def e_copy(i):
        rows = pl.ds(pl.multiple_of(i * PB, PB), PB)
        return rcopy(ef.at[rows], sibe.at[rows], e_s.at[i], e_r.at[i], sib)

    def e_block(which, n):
        return which * (NPB // 2) + lax.rem(n + z // 2 + 2, NPB // 2)

    def e_step(i):
        base = pl.multiple_of(i * PB, PB)
        parts = []
        for j in range(NSG):
            w = endw[pl.ds(i * NSG + j, 1), :]
            xt = xst[pl.ds(pl.multiple_of(base + j * HD, HD), HD), :]
            parts.append((xt.astype(F32) * w).astype(BF16))
        e = jnp.dot(jnp.concatenate(parts, axis=0), keys[...], preferred_element_type=F32)
        ef[pl.ds(base, PB), :] = e
        e_copy(i).start()

    def e_other(n, _):
        e_step(e_block(1 - core, n))
        return 0

    lax.fori_loop(0, NPB // 2, e_other, 0)

    xrow = lax.broadcasted_iota(jnp.int32, (16, 128), 0) // 3

    def encode(blocks):
        q = []
        ex = jnp.zeros((16, 128), F32)
        for k in range(NSG):
            top = jnp.max(jnp.abs(blocks[k]), axis=0, keepdims=True)
            e = jnp.ceil(jnp.log2(jnp.maximum(top, 1e-30))) - 14.0
            q.append(jnp.floor(blocks[k] * (1.0 / jnp.exp2(e)) + 0.5))
            ex = jnp.where(xrow == k, e, ex)
        return jnp.concatenate(q + [ex], axis=0).astype(jnp.int32).astype(jnp.int16)

    def decode(ref):
        ex = jnp.exp2(ref[PR:XP, :].astype(jnp.int32).astype(F32))
        return [
            ref[k * SG : (k + 1) * SG, :].astype(jnp.int32).astype(F32) * ex[3 * k : 3 * k + 1]
            for k in range(NSG)
        ]

    def head_of(o, k):
        return core * (HEADS // 2) + (o * NSG + k) // 2

    def p1_copy(to, frm):
        return rcopy(p1s.at[to], p1r.at[frm], p1_s.at[to], p1_r.at[frm], at(x, to, core))

    def chip_step(o):
        blocks = []
        for k in range(NSG):
            rows = pl.ds(pl.multiple_of(core * HALF + o * PR + k * SG, SG), SG)
            own, other = ef[rows, :], sibe[rows, :]
            h = pl.ds(head_of(o, k), 1)
            low = jnp.where(core == 0, own, other)
            high = jnp.where(core == 0, other, own)
            d = jnp.where(core == 0, theta[1, h, :], theta[0, h, :])
            blocks.append(low * d + high)
        p1s[o] = encode(blocks)

        @pl.when(o != z)
        def _():
            p1_copy(o, z).start()

        @pl.when(o == z)
        def _():
            p1r[o] = p1s[o]

    def e_mine(n, _):
        i = e_block(core, n)
        e_step(i)
        e_copy(i).wait_recv()
        for m in range(2):
            chip_step(2 * lax.rem(n + z // 2 + 2, NPB // 2) + m)
        return 0

    lax.fori_loop(0, NPB // 2, e_mine, 0)

    over_z(lambda o: dz_copy(o, o).wait_recv())
    pair = [dtab[2 * j] * dtab[2 * j + 1] for j in range(NZ // 2)]
    quad = [pair[0] * pair[1], pair[2] * pair[3]]
    dline[x] = quad[0] * quad[1]
    over_x(lambda o: dx_copy(o, x).start())


    me = core * NZ + z

    def l_copy(lvl, src, o, frm):
        return rcopy(
            src, lbuf.at[lvl, core * NZ + frm], l_s.at[lvl, o], l_r.at[lvl, frm], at(x, o, core)
        )

    def l1_copy(o):
        return rcopy(
            p1s.at[o],
            lbuf.at[0, core * NZ + o],
            l1_s.at[o],
            l_r.at[0, o],
            at(x, zpeer(1), core),
        )

    def l1_direct(do):
        for d in range(4):
            do(l1_copy(zpeer(NZ - d)))


    s_t = lax.dot_general(
        keys[...], quer[...], (((1,), (1,)), ((), ())), preferred_element_type=F32
    )
    rowi = lax.broadcasted_iota(jnp.int32, (TOK, TOK), 0)
    coli = lax.broadcasted_iota(jnp.int32, (TOK, TOK), 1)
    ok = (rowi <= coli) & (seg_col == seg_row)
    sct[...] = jnp.where(ok, s_t, 0.0)

    def local_heads(i, _):
        rolled = pltpu.roll(cumt[...], lax.rem(128 - i * HPB, 128), 1)
        for j in range(HPB):
            h = i * HPB + j
            rows = pl.ds(pl.multiple_of(h * HD, HD), HD)
            ccol = rolled[:, j : j + 1]
            crow = cum[pl.ds(h, 1), :]

            def lam_row(l, lo):
                return lam[l, pl.ds(h, 1), :][:, lo : lo + 128]

            def picked(lo):
                p = jnp.broadcast_to(lam_row(7, lo), (128, 128))
                for l in range(7):
                    p = jnp.where(lev[...] == l, lam_row(l, lo), p)
                return p

            def mix(slo, tlo, pick):
                gap = crow[:, tlo : tlo + 128] - ccol[slo : slo + 128]
                decay = jnp.exp(jnp.minimum(gap, 0.0))
                return (sct[slo : slo + 128, tlo : tlo + 128] * pick * decay).astype(BF16)

            m00 = mix(0, 0, picked(0))
            m01 = mix(0, 128, lam_row(8, 128))
            m11 = mix(128, 128, picked(128))
            xs = xst[rows, :]
            left = jnp.dot(xs[:, 0:128], m00, preferred_element_type=F32)
            right = jnp.dot(xs, jnp.concatenate([m01, m11], axis=0), preferred_element_type=F32)
            acc[rows, :] = jnp.concatenate([left, right], axis=1) + skip[h] * xs.astype(F32)
        return 0

    pair = [dtab[2 * j] * dtab[2 * j + 1] for j in range(NZ // 2)]
    quad = [pair[0] * pair[1], pair[2] * pair[3]]
    one = jnp.ones((HEADS, 128), F32)
    pbuf[1] = jnp.where(core == 1, theta[1], one)
    below = jnp.where(lax.rem(z, 2) == 1, dtab[jnp.maximum(z - 1, 0)], one)
    pbuf[2] = pbuf[1] * below
    pbuf[3] = pbuf[2] * jnp.where(
        lax.rem(z // 2, 2) == 1, jnp.where(z >= 4, pair[2], pair[0]), one
    )
    pbuf[4] = pbuf[3] * jnp.where(z >= 4, quad[0], one)

    in_copies[1].wait()
    lax.fori_loop(0, LOCAL_A, local_heads, 0)

    over_z(lambda o: p1_copy(o, o).wait_recv())
    cs = [decode(p1r.at[j]) for j in range(NZ)]
    b01, b45, b03, b07 = [], [], [], []
    for k in range(NSG):
        h = pl.ds(head_of(z, k), 1)
        d = [dtab[j, h, :] for j in range(NZ)]
        pr = [cs[2 * j][k] * d[2 * j + 1] + cs[2 * j + 1][k] for j in range(NZ // 2)]
        lo = pr[0] * (d[2] * d[3]) + pr[1]
        hi = pr[2] * (d[6] * d[7]) + pr[3]
        b01.append(pr[0])
        b45.append(pr[2])
        b03.append(lo)
        b07.append(lo * (d[4] * d[5] * d[6] * d[7]) + hi)
    osnd[3] = encode(b07)

    def x_copy(to, frm):
        return rcopy(osnd.at[3], tr.at[frm], x_s.at[to], x_r.at[frm], at(to, z, core))

    def x_to(o):
        return (o > x) & ((o < 3) | (x == 2))

    def send_x(o):
        @pl.when(x_to(o))
        def _():
            x_copy(o, x).start()

    over_x(send_x)
    osnd[2] = encode(b03)
    osnd[0] = encode(b01)
    osnd[1] = encode(b45)

    def sib_copy(lvl, o):
        dst = lbuf.at[lvl, core * NZ + o]
        return rcopy(dst, dst, sib_s.at[lvl, o], sib_r.at[lvl, o], sib)

    def sib_wait(lvl, o):
        dst = lbuf.at[lvl, (1 - core) * NZ + o]
        rcopy(dst, dst, sib_s.at[lvl, o], sib_r.at[lvl, o], sib).wait_recv()

    def bit(v, b):
        return lax.rem(v // 2**b, 2) == 1

    def keep(lvl, src):
        lbuf[lvl, me] = src
        sib_copy(lvl, z).start()

    def mir(o):
        return jnp.where(z >= 6, lax.rem(11 - o, NZ), o)

    l3_to = jnp.where(z >= 2, 4, 7)
    l3_end = (z == 4) | (z == 7)
    l3_mid = (z == 5) | (z == 6)

    def l3_own(do):
        @pl.when(z < 4)
        def _():
            do(lambda: l_copy(2, osnd.at[2], l3_to, z))

        @pl.when(z >= 4)
        def _():
            do(lambda: l_copy(2, osnd.at[2], jnp.where(l3_end, mir(5), mir(4)), z))
            do(lambda: l_copy(2, osnd.at[2], mir(6), z))

    def l3_on(slot, o, to):
        dst = lbuf.at[2, core * NZ + o]
        return rcopy(dst, dst, r3_s.at[slot, o], l_r.at[2, o], at(x, to, core))

    def l3_in(o):
        l_copy(2, lbuf.at[2, me], o, o).wait_recv()

    def l3_first():
        @pl.when(l3_end)
        def _():
            for q in (3, 2):
                o = mir(q)
                l3_in(o)
                l3_on(0, o, mir(5)).start()
                l3_on(1, o, mir(6)).start()
                sib_copy(2, o).start()

    def l3_middle():
        @pl.when(l3_mid)
        def _():
            for q in (6, 7, 0, 1):
                o = mir(q)
                l3_in(o)
                l3_on(0, o, mir(4)).start()
                sib_copy(2, o).start()

    def l3_rest():
        @pl.when(l3_mid)
        def _():
            for q in (4, 3, 2):
                o = mir(q)
                l3_in(o)
                sib_copy(2, o).start()

        @pl.when(l3_end)
        def _():
            for q in (5, 6, 7, 0, 1):
                o = mir(q)
                l3_in(o)
                sib_copy(2, o).start()

    def l3_on_done():
        @pl.when(l3_end)
        def _():
            for q in (3, 2):
                l3_on(0, mir(q), mir(5)).wait_send()
                l3_on(1, mir(q), mir(6)).wait_send()

        @pl.when(l3_mid)
        def _():
            for q in (6, 7, 0, 1):
                l3_on(0, mir(q), mir(4)).wait_send()

    def l2_own(do):
        for p in (2, 6):
            r = lax.rem(z + NZ - p, NZ)
            to = jnp.where((r == 1) | (r >= 5), p, p + 1)
            do(lambda to=to, p=p: l_copy(1, osnd.at[p // 4], to, z))

    l2_other = jnp.where(lax.rem(z, 2) == 0, z + 1, z - 1)

    def l2_off(d):
        return lax.rem(jnp.where(lax.rem(z, 2) == 0, z + NZ - d, z + d), NZ)

    def l2_on(o):
        dst = lbuf.at[1, core * NZ + o]
        return rcopy(dst, dst, r2_s.at[o], l_r.at[1, o], at(x, l2_other, core))

    def l2_in(o):
        l_copy(1, lbuf.at[1, me], o, o).wait_recv()

    def l2_first():
        @pl.when(bit(z, 1))
        def _():
            for d in (1, 2, 3):
                l2_in(l2_off(d))
                l2_on(l2_off(d)).start()
                sib_copy(1, l2_off(d)).start()

    def l2_rest():
        @pl.when(bit(z, 1))
        def _():
            for d in (7, 6, 5, 4):
                l2_in(l2_off(d))
                sib_copy(1, l2_off(d)).start()

    l3_own(lambda c: c().start())
    l2_own(lambda c: c().start())

    def l1_owner(do):
        for d in (1, 2, 3):
            to = zpeer(NZ - d)

            @pl.when(lax.rem(to, 2) == 1)
            def _(to=to):
                do(
                    lambda: l_copy(
                        0, p1r.at[lax.rem(to + NZ - 1, NZ)], to, z
                    )
                )

    @pl.when(lax.rem(z, 2) == 0)
    def _():
        l1_direct(lambda c: c.start())

    l1_owner(lambda c: c().start())

    @pl.when(lax.rem(z, 2) == 1)
    def _():
        keep(0, p1r[jnp.maximum(z - 1, 0)])

    @pl.when(z >= 4)
    def _():
        keep(2, osnd[2])

    @pl.when(bit(z, 1))
    def _():
        keep(1, osnd[z // 4])

    def sib_all(lvl):
        def go(o, _):
            sib_wait(lvl, o)
            return 0

        lax.fori_loop(0, NZ, go, 0)

    def far(level):
        def body(i, _):
            base = pl.multiple_of(i * PB, PB)
            if level == 0:
                state = sibe[pl.ds(base, PB), :].astype(BF16)
            else:
                parts = []
                for m in range(2):
                    v = decode(lbuf.at[level - 1, 2 * i + m])
                    for k in range(NSG):
                        p = pbuf[level, pl.ds(i * NSG + (m * NSG + k) // 2, 1), :]
                        parts.append((v[k] * p).astype(BF16))
                state = jnp.concatenate(parts, axis=0)
            read = lax.dot_general(
                state, quer[...], (((1,), (1,)), ((), ())), preferred_element_type=F32
            )
            for j in range(NSG):
                h = pl.ds(i * NSG + j, 1)
                coef = lam[9 + level, h, :] * entry[h, :]
                rows = pl.ds(pl.multiple_of(base + j * HD, HD), HD)
                acc[rows, :] = acc[rows, :] + read[j * HD : (j + 1) * HD] * coef
            return 0

        lax.fori_loop(0, NPB, body, 0)

    def gate_block(i, _):
        cols = pl.ds(pl.multiple_of(i * BR, BR), BR)
        v = gate[:, cols].astype(F32)
        gt[cols, :] = (v * (1.0 / (1.0 + jnp.exp(-v)))).T
        return 0

    lax.fori_loop(LOCAL_A, NB, local_heads, 0)
    in_copies[2].wait()
    lax.fori_loop(0, NB, gate_block, 0)

    def wait_e2(n, _):
        e_copy((1 - core) * (NPB // 2) + n).wait_recv()
        return 0

    lax.fori_loop(0, NPB // 2, wait_e2, 0)

    @pl.when(core == 1)
    def _():
        far(0)

    over_x(lambda o: dx_copy(o, o).wait_recv())
    pbuf[5] = pbuf[4] * jnp.where(lax.rem(x, 2) == 1, dline[jnp.maximum(x - 1, 0)], one)

    def x_in(frm):
        x_copy(frm, frm).wait_recv()

    NEAR = (2, 6, 1, 7)

    def spread(lvl, src):
        for d in NEAR:
            l_copy(lvl, src, zpeer(d), z).start()

    def r_copy(lvl, d, frm):
        dst = lbuf.at[lvl, core * NZ + frm]
        to = zpeer(d)
        return rcopy(dst, dst, r_s.at[to], l_r.at[lvl, frm], at(x, to, core))

    def up_copy(src, frm):
        return rcopy(
            src, lbuf.at[4, core * NZ + frm], up_s.at[frm], l_r.at[4, frm], at(xpeer(1), z, core)
        )

    def gather(lvl, up, first):
        def arrived(frm):
            l_copy(lvl, lbuf.at[lvl, me], frm, frm).wait_recv()

        def hand_on(frm):
            sib_copy(lvl, frm).start()
            if up:
                up_copy(lbuf.at[lvl, core * NZ + frm], frm).start()

        def pull(d):
            arrived(zpeer(d))
            hand_on(zpeer(d))

        if not first:
            for d in (1, 7, 3, 5, 4):
                pull(d)
            return
        arrived(zpeer(6))
        r_copy(lvl, 1, zpeer(6)).start()

        hand_on(zpeer(6))
        arrived(zpeer(2))
        r_copy(lvl, 7, zpeer(2)).start()
        r_copy(lvl, 6, zpeer(2)).start()

        hand_on(zpeer(2))

    def send_l4(frm):
        spread(3, tr.at[frm])
        keep(3, tr[frm])

    def send_l5():
        t0, t1 = decode(tr.at[0]), decode(tr.at[1])
        osnd[4] = encode(
            [t0[k] * dline[1, pl.ds(head_of(z, k), 1), :] + t1[k] for k in range(NSG)]
        )
        spread(4, osnd.at[4])
        up_copy(osnd.at[4], z).start()
        keep(4, osnd[4])

    @pl.when(x == 1)
    def _():
        x_in(0)
        send_l4(0)

    @pl.when(x == 3)
    def _():
        x_in(2)
        send_l4(2)

    @pl.when(x == 2)
    def _():
        x_in(1)
        x_in(0)
        send_l5()

    l3_first()
    l2_first()

    @pl.when(lax.rem(x, 2) == 1)
    def _():
        gather(3, False, True)

    @pl.when(x == 2)
    def _():
        gather(4, True, True)

    l3_middle()

    @pl.when(lax.rem(x, 2) == 1)
    def _():
        gather(3, False, False)

    @pl.when(x == 2)
    def _():
        gather(4, True, False)

    @pl.when(lax.rem(z, 2) == 1)
    def _():
        def go(o):
            l_copy(0, lbuf.at[0, me], o, o).wait_recv()
            sib_copy(0, o).start()

        over_z(go)

    l3_rest()
    l2_rest()

    @pl.when(lax.rem(z, 2) == 1)
    def _():
        sib_all(0)
        far(1)

    @pl.when(bit(z, 1))
    def _():
        sib_all(1)
        far(2)

    @pl.when(z >= 4)
    def _():
        sib_all(2)
        far(3)

    @pl.when(x == 3)
    def _():
        def go(o, _):
            up_copy(osnd.at[4], o).wait_recv()
            sib_copy(4, o).start()
            return 0

        lax.fori_loop(0, NZ, go, 0)

    @pl.when(lax.rem(x, 2) == 1)
    def _():
        sib_all(3)
        far(4)

    @pl.when(x >= 2)
    def _():
        sib_all(4)
        far(5)

    def gate_step(i, ssq):
        rows = pl.ds(pl.multiple_of(i * BR, BR), BR)
        v = acc[rows, :] * gt[rows, :]
        acc[rows, :] = v
        return ssq + jnp.sum((v * v).reshape(BR // 8, 8, TOK), axis=0)

    ssq = lax.fori_loop(0, NB, gate_step, jnp.zeros((8, TOK), F32))
    scale = lax.rsqrt(jnp.sum(ssq, axis=0, keepdims=True) * (1.0 / WIDTH) + EPS)

    def out_step(i, _):
        cols = pl.ds(pl.multiple_of(i * BR, BR), BR)
        v = (acc[cols, :] * scale).T
        out[:, cols] = (v * ng[cols].reshape(1, BR)).astype(BF16)
        return 0

    lax.fori_loop(0, NB, out_step, 0)

    halo_copy.wait_send()
    th_copy.wait_send()

    def e_done(i, _):
        e_copy(i).wait_send()
        return 0

    lax.fori_loop(0, NPB, e_done, 0)
    over_z(lambda o: dz_copy(o, z).wait_send())
    over_z(lambda o: p1_copy(o, z).wait_send())
    over_x(lambda o: dx_copy(o, x).wait_send())

    def x_done(o):
        @pl.when(x_to(o))
        def _():
            x_copy(o, x).wait_send()

    over_x(x_done)

    l3_own(lambda c: c().wait_send())
    l3_on_done()
    l2_own(lambda c: c().wait_send())

    @pl.when(bit(z, 1))
    def _():
        for d in (1, 2, 3):
            l2_on(l2_off(d)).wait_send()

    def spread_done(lvl):
        for d in NEAR:
            l_copy(lvl, osnd.at[4], zpeer(d), z).wait_send()
        for d in (1, 7, 6):
            r_copy(lvl, d, z).wait_send()

    pl.when(lax.rem(x, 2) == 1)(lambda: spread_done(3))

    @pl.when(x == 2)
    def _():
        spread_done(4)

        def go(o, _):
            up_copy(osnd.at[4], o).wait_send()
            return 0

        lax.fori_loop(0, NZ, go, 0)

    def sib_done(lvl):
        def go(o, _):
            sib_copy(lvl, o).wait_send()
            return 0

        lax.fori_loop(0, NZ, go, 0)

    @pl.when(lax.rem(z, 2) == 0)
    def _():
        l1_direct(lambda c: c.wait_send())

    l1_owner(lambda c: c().wait_send())
    pl.when(lax.rem(z, 2) == 1)(lambda: sib_done(0))
    pl.when(bit(z, 1))(lambda: sib_done(1))
    pl.when(z >= 4)(lambda: sib_done(2))
    pl.when(lax.rem(x, 2) == 1)(lambda: sib_done(3))
    pl.when(x >= 2)(lambda: sib_done(4))


def per_device(
    mixed_input,
    conv_weight,
    conv_bias,
    gate_input,
    log_decay,
    level_weights,
    skip_gain,
    norm_gain,
    seg_lengths,
):
    vmem = pl.BlockSpec(memory_space=pltpu.VMEM)
    hbm = pl.BlockSpec(memory_space=pl.ANY)
    smem = pl.BlockSpec(memory_space=pltpu.SMEM)
    dma = pltpu.SemaphoreType.DMA
    return pl.pallas_call(
        kernel,
        out_shape=pltpu.VMEM((TOK, WIDTH), BF16),
        in_specs=[hbm, hbm, vmem, hbm] + [vmem] * 3 + [smem] * 2,
        out_specs=vmem,
        scratch_shapes=[
            pltpu.VMEM((TOK, CH), BF16),
            pltpu.VMEM((TOK, WIDTH), BF16),
            pltpu.VMEM((20, HEADS, TOK), F32),
            pltpu.VMEM((HALO, CH), BF16),
            pltpu.VMEM((TOK + 8, BR), F32),
            pltpu.VMEM((TOK, CH), F32),
            pltpu.VMEM((WIDTH, TOK), BF16),
            pltpu.VMEM((TOK, STATE), BF16),
            pltpu.VMEM((TOK, STATE), BF16),
            pltpu.VMEM((WIDTH, STATE), F32),
            pltpu.VMEM((WIDTH, STATE), F32),
            pltpu.VMEM((NZ, XP, STATE), jnp.int16),
            pltpu.VMEM((NZ, XP, STATE), jnp.int16),
            pltpu.VMEM((5, XP, STATE), jnp.int16),
            pltpu.VMEM((NX, XP, STATE), jnp.int16),
            pltpu.VMEM((5, 2 * NZ, XP, STATE), jnp.int16),
            pltpu.VMEM((NZ, HEADS, 128), F32),
            pltpu.VMEM((NX, HEADS, 128), F32),
            pltpu.VMEM((2, HEADS, 128), F32),
            pltpu.VMEM((6, HEADS, 128), F32),
            pltpu.VMEM((HEADS, TOK), F32),
            pltpu.VMEM((TOK, 128), F32),
            pltpu.VMEM((HEADS, TOK), F32),
            pltpu.VMEM((HEADS, TOK), F32),
            pltpu.VMEM((TOK, TOK), F32),
            pltpu.VMEM((128, 128), jnp.int32),
            pltpu.VMEM((WIDTH, TOK), F32),
            pltpu.VMEM((WIDTH, TOK), F32),
            dma((3,)),
            dma,
            dma,
            dma,
            dma,
            dma((NPB,)),
            dma((NPB,)),
            dma((NZ,)),
            dma((NZ,)),
            dma((NX,)),
            dma((NX,)),
            dma((NZ,)),
            dma((NZ,)),
            dma((5, NZ)),
            dma((5, NZ)),
            dma((NZ,)),
            dma((NZ,)),
            dma((2, NZ)),
            dma((NZ,)),
            dma((NZ,)),
            dma((NX,)),
            dma((NX,)),
            dma((5, NZ)),
            dma((5, NZ)),
        ],
        compiler_params=pltpu.CompilerParams(
            collective_id=0, has_side_effects=True, vmem_limit_bytes=60 * 1024 * 1024
        ),
        name="layer",
    )(
        mixed_input,
        gate_input,
        log_decay,
        jnp.transpose(level_weights, (1, 0, 2)),
        conv_weight,
        conv_bias,
        norm_gain,
        skip_gain,
        seg_lengths,
    )


def solution(mesh):
    in_specs = (
        P(("batch", "group"), None),
        P(),
        P(),
        P(("batch", "group"), None),
        P(None, ("batch", "group")),
        P(None, None, ("batch", "group")),
        P(),
        P(),
        P("batch"),
    )
    out_specs = P(("batch", "group"), None)
    return jax.shard_map(
        per_device, mesh=mesh, in_specs=in_specs, out_specs=out_specs, check_vma=False
    )
```

```python
import jax
import jax.numpy as jnp
from jax import lax
from jax.experimental import pallas as pl
from jax.experimental.pallas import tpu as pltpu
from jax.sharding import PartitionSpec as P

EPS = 1e-05
F32 = jnp.float32
BF16 = jnp.bfloat16
MESH = pl.DeviceIdType.MESH

TOK = 256
WIDTH = 2560
HEADS = 40
HD = 64
STATE = 128
CH = 2816
TAPS = 4
NX, NZ = 4, 8
HALF = WIDTH // 2
HALO = 16
PR = HALF // NZ
SG = 32
NSG = PR // SG
XP = PR + 16
PB = 2 * PR
NPB = WIDTH // PB
BR = 256
NB = WIDTH // BR
HPB = BR // HD
LOCAL_A = 8
CONV_A = 4


def kernel(
    mixed_h,
    gate_h,
    ld,
    lam_h,
    cw,
    cb,
    ng,
    skip,
    segl,
    out,
    mixed,
    gate,
    lam,
    halo,
    pad,
    act,
    xst,
    keys,
    quer,
    ef,
    sibe,
    p1s,
    p1r,
    osnd,
    tr,
    lbuf,
    dtab,
    dline,
    theta,
    pbuf,
    cum,
    cumt,
    endw,
    entry,
    sct,
    lev,
    acc,
    gt,
    in_s,
    halo_s,
    halo_r,
    th_s,
    th_r,
    e_s,
    e_r,
    dz_s,
    dz_r,
    dx_s,
    dx_r,
    p1_s,
    p1_r,
    l_s,
    l_r,
    l1_s,
    r2_s,
    r3_s,
    r_s,
    up_s,
    x_s,
    x_r,
    sib_s,
    sib_r,
):
    g = lax.axis_index("group")
    core = lax.rem(g, 2)
    z = lax.rem(g // 2, NZ)
    x = g // (2 * NZ)
    ngroups = 2 * NZ * NX

    def at(xx, zz, cc):
        return (xx * NZ + zz) * 2 + cc

    sib = at(x, z, 1 - core)
    gnext = lax.rem(g + 1, ngroups)
    gprev = lax.rem(g + ngroups - 1, ngroups)

    def zpeer(d):
        return lax.rem(z + d, NZ)

    def xpeer(d):
        return lax.rem(x + d, NX)

    barrier = pltpu.get_barrier_semaphore()

    def hello(peer):
        pl.semaphore_signal(barrier, inc=1, device_id={"group": peer}, device_id_type=MESH)

    for d in range(1, NZ):
        hello(at(x, zpeer(d), core))
    for d in range(1, NX):
        hello(at(xpeer(d), z, core))
    for peer in (sib, gnext, gprev):
        hello(peer)
    n_hello = NZ - 1 + NX - 1 + 3

    in_copies = [
        pltpu.make_async_copy(mixed_h, mixed, in_s.at[0]),
        pltpu.make_async_copy(lam_h, lam, in_s.at[1]),
        pltpu.make_async_copy(gate_h, gate, in_s.at[2]),
    ]
    for cp in in_copies:
        cp.start()

    def rcopy(src, dst, ss, rs, peer):
        return pltpu.make_async_remote_copy(
            src_ref=src,
            dst_ref=dst,
            send_sem=ss,
            recv_sem=rs,
            device_id={"group": peer},
            device_id_type=MESH,
        )

    first = g * TOK
    b1 = segl[0]
    b2 = segl[0] + segl[1]

    def seg_of(pos):
        s = (pos >= b1).astype(jnp.int32) + (pos >= b2).astype(jnp.int32)
        return jnp.where(pos >= 0, s, -1)

    lane_pos = first + lax.broadcasted_iota(jnp.int32, (8, TOK), 1)[0:1]
    seg_row = seg_of(lane_pos)
    last_row = seg_of(jnp.full((1, TOK), first + TOK - 1, jnp.int32))
    prev_row = seg_of(jnp.full((1, TOK), first - 1, jnp.int32))

    c = ld[...]
    lane = lax.broadcasted_iota(jnp.int32, (HEADS, TOK), 1)
    step = 1
    while step < TOK:
        c = c + jnp.where(lane >= step, pltpu.roll(c, step, 1), 0.0)
        step *= 2
    cum[...] = c
    c_end = c[:, TOK - 1 : TOK]
    endw[...] = jnp.exp(c_end - c) * (seg_row == last_row).astype(F32)
    entry[...] = jnp.exp(c) * (seg_row == prev_row).astype(F32)
    theta[0] = jnp.broadcast_to(jnp.exp(c_end), (HEADS, 128)) * (last_row == prev_row).astype(F32)[
        :, 0:128
    ]
    cpad = jnp.concatenate([c, jnp.zeros((128 - HEADS, TOK), F32)], axis=0)
    cumt[...] = jnp.concatenate([cpad[:, 0:128].T, cpad[:, 128:256].T], axis=0)

    si = lax.broadcasted_iota(jnp.int32, (128, 128), 0)
    ti = lax.broadcasted_iota(jnp.int32, (128, 128), 1)
    diff = si ^ ti
    lv = jnp.zeros((128, 128), jnp.int32)
    for b in range(7):
        lv = lv + (diff >= 2**b).astype(jnp.int32)
    lev[...] = lv

    col_pos = first + lax.broadcasted_iota(jnp.int32, (TOK, 256), 0)
    seg_col = seg_of(col_pos)
    same = [None] + [seg_of(col_pos - t) == seg_col for t in range(1, TAPS)]

    def taps(cols, rows, cur):
        total = cb[cols].reshape(1, BR) + cw[0:1, cols] * cur
        for t in range(1, TAPS):
            piece = pad[8 - t : 8 - t + rows, :]
            total = total + cw[t : t + 1, cols] * jnp.where(same[t][0:rows], piece, 0.0)
        return total * (1.0 / (1.0 + jnp.exp(-total)))

    pad[0:8, :] = jnp.zeros((8, BR), F32)

    def conv_rows(i, _):
        cols = pl.ds(pl.multiple_of(i * BR, BR), BR)
        cur = mixed[:, cols].astype(F32)
        pad[8 : 8 + TOK, :] = cur
        act[:, cols] = taps(cols, TOK, cur)
        return 0

    def conv_first(i, _):
        cols = pl.ds(pl.multiple_of(i * BR, BR), BR)
        cur = mixed[0:16, cols].astype(F32)[0:8]
        pad[8:16, :] = cur
        pad[0:8, :] = halo[:, cols].astype(F32)[8:16]
        act[0:8, cols] = taps(cols, 8, cur)
        return 0

    in_copies[0].wait()
    lax.fori_loop(0, CONV_A, conv_rows, 0)
    pl.semaphore_wait(barrier, n_hello)

    halo_copy = rcopy(mixed.at[pl.ds(TOK - HALO, HALO)], halo, halo_s, halo_r, gnext)
    halo_copy.start()
    th_copy = rcopy(theta.at[0], theta.at[1], th_s, th_r, sib)
    th_copy.start()
    lax.fori_loop(CONV_A, CH // BR, conv_rows, 0)

    th_copy.wait_recv()
    dtab[z] = theta[0] * theta[1]

    def dz_copy(to, frm):
        return rcopy(dtab.at[frm], dtab.at[frm], dz_s.at[to], dz_r.at[frm], at(x, to, core))

    def dx_copy(to, frm):
        return rcopy(dline.at[frm], dline.at[frm], dx_s.at[to], dx_r.at[frm], at(to, z, core))

    def over_z(f):
        def go(d, _):
            f(zpeer(d))
            return 0

        lax.fori_loop(1, NZ, go, 0)

    def over_x(f):
        def go(d, _):
            f(xpeer(d))
            return 0

        lax.fori_loop(1, NX, go, 0)

    over_z(lambda o: dz_copy(o, z).start())

    halo_copy.wait_recv()
    lax.fori_loop(0, CH // BR, conv_first, 0)
    keys[...] = act[:, WIDTH : WIDTH + STATE].astype(BF16)
    quer[...] = act[:, WIDTH + STATE : CH].astype(BF16)

    def turn(i, _):
        base = pl.multiple_of(i * BR, BR)
        xst[pl.ds(base, BR), :] = act[:, pl.ds(base, BR)].T.astype(BF16)
        return 0

    lax.fori_loop(0, NB, turn, 0)

    def e_copy(i):
        rows = pl.ds(pl.multiple_of(i * PB, PB), PB)
        return rcopy(ef.at[rows], sibe.at[rows], e_s.at[i], e_r.at[i], sib)

    def e_block(which, n):
        return which * (NPB // 2) + lax.rem(n + z // 2 + 2, NPB // 2)

    def e_step(i):
        base = pl.multiple_of(i * PB, PB)
        parts = []
        for j in range(NSG):
            w = endw[pl.ds(i * NSG + j, 1), :]
            xt = xst[pl.ds(pl.multiple_of(base + j * HD, HD), HD), :]
            parts.append((xt.astype(F32) * w).astype(BF16))
        e = jnp.dot(jnp.concatenate(parts, axis=0), keys[...], preferred_element_type=F32)
        ef[pl.ds(base, PB), :] = e
        e_copy(i).start()

    def e_other(n, _):
        e_step(e_block(1 - core, n))
        return 0

    lax.fori_loop(0, NPB // 2, e_other, 0)

    xrow = lax.broadcasted_iota(jnp.int32, (16, 128), 0) // 3

    def encode(blocks):
        q = []
        ex = jnp.zeros((16, 128), F32)
        for k in range(NSG):
            top = jnp.max(jnp.abs(blocks[k]), axis=0, keepdims=True)
            e = jnp.ceil(jnp.log2(jnp.maximum(top, 1e-30))) - 14.0
            q.append(jnp.floor(blocks[k] * (1.0 / jnp.exp2(e)) + 0.5))
            ex = jnp.where(xrow == k, e, ex)
        return jnp.concatenate(q + [ex], axis=0).astype(jnp.int32).astype(jnp.int16)

    def decode(ref):
        ex = jnp.exp2(ref[PR:XP, :].astype(jnp.int32).astype(F32))
        return [
            ref[k * SG : (k + 1) * SG, :].astype(jnp.int32).astype(F32) * ex[3 * k : 3 * k + 1]
            for k in range(NSG)
        ]

    def head_of(o, k):
        return core * (HEADS // 2) + (o * NSG + k) // 2

    def p1_copy(to, frm):
        return rcopy(p1s.at[to], p1r.at[frm], p1_s.at[to], p1_r.at[frm], at(x, to, core))

    def chip_step(o):
        blocks = []
        for k in range(NSG):
            rows = pl.ds(pl.multiple_of(core * HALF + o * PR + k * SG, SG), SG)
            own, other = ef[rows, :], sibe[rows, :]
            h = pl.ds(head_of(o, k), 1)
            low = jnp.where(core == 0, own, other)
            high = jnp.where(core == 0, other, own)
            d = jnp.where(core == 0, theta[1, h, :], theta[0, h, :])
            blocks.append(low * d + high)
        p1s[o] = encode(blocks)

        @pl.when(o != z)
        def _():
            p1_copy(o, z).start()

        @pl.when(o == z)
        def _():
            p1r[o] = p1s[o]

    def e_mine(n, _):
        i = e_block(core, n)
        e_step(i)
        e_copy(i).wait_recv()
        for m in range(2):
            chip_step(2 * lax.rem(n + z // 2 + 2, NPB // 2) + m)
        return 0

    lax.fori_loop(0, NPB // 2, e_mine, 0)

    over_z(lambda o: dz_copy(o, o).wait_recv())
    pair = [dtab[2 * j] * dtab[2 * j + 1] for j in range(NZ // 2)]
    quad = [pair[0] * pair[1], pair[2] * pair[3]]
    dline[x] = quad[0] * quad[1]
    over_x(lambda o: dx_copy(o, x).start())


    me = core * NZ + z

    def l_copy(lvl, src, o, frm):
        return rcopy(
            src, lbuf.at[lvl, core * NZ + frm], l_s.at[lvl, o], l_r.at[lvl, frm], at(x, o, core)
        )

    def l1_copy(o):
        return rcopy(
            p1s.at[o],
            lbuf.at[0, core * NZ + o],
            l1_s.at[o],
            l_r.at[0, o],
            at(x, zpeer(1), core),
        )

    def l1_direct(do):
        for d in range(4):
            do(l1_copy(zpeer(NZ - d)))


    s_t = lax.dot_general(
        keys[...], quer[...], (((1,), (1,)), ((), ())), preferred_element_type=F32
    )
    rowi = lax.broadcasted_iota(jnp.int32, (TOK, TOK), 0)
    coli = lax.broadcasted_iota(jnp.int32, (TOK, TOK), 1)
    ok = (rowi <= coli) & (seg_col == seg_row)
    sct[...] = jnp.where(ok, s_t, 0.0)

    def local_heads(i, _):
        rolled = pltpu.roll(cumt[...], lax.rem(128 - i * HPB, 128), 1)
        for j in range(HPB):
            h = i * HPB + j
            rows = pl.ds(pl.multiple_of(h * HD, HD), HD)
            ccol = rolled[:, j : j + 1]
            crow = cum[pl.ds(h, 1), :]

            def lam_row(l, lo):
                return lam[l, pl.ds(h, 1), :][:, lo : lo + 128]

            def picked(lo):
                p = jnp.broadcast_to(lam_row(7, lo), (128, 128))
                for l in range(7):
                    p = jnp.where(lev[...] == l, lam_row(l, lo), p)
                return p

            def mix(slo, tlo, pick):
                gap = crow[:, tlo : tlo + 128] - ccol[slo : slo + 128]
                decay = jnp.exp(jnp.minimum(gap, 0.0))
                return (sct[slo : slo + 128, tlo : tlo + 128] * pick * decay).astype(BF16)

            m00 = mix(0, 0, picked(0))
            m01 = mix(0, 128, lam_row(8, 128))
            m11 = mix(128, 128, picked(128))
            xs = xst[rows, :]
            left = jnp.dot(xs[:, 0:128], m00, preferred_element_type=F32)
            right = jnp.dot(xs, jnp.concatenate([m01, m11], axis=0), preferred_element_type=F32)
            acc[rows, :] = jnp.concatenate([left, right], axis=1) + skip[h] * xs.astype(F32)
        return 0

    pair = [dtab[2 * j] * dtab[2 * j + 1] for j in range(NZ // 2)]
    quad = [pair[0] * pair[1], pair[2] * pair[3]]
    one = jnp.ones((HEADS, 128), F32)
    pbuf[1] = jnp.where(core == 1, theta[1], one)
    below = jnp.where(lax.rem(z, 2) == 1, dtab[jnp.maximum(z - 1, 0)], one)
    pbuf[2] = pbuf[1] * below
    pbuf[3] = pbuf[2] * jnp.where(
        lax.rem(z // 2, 2) == 1, jnp.where(z >= 4, pair[2], pair[0]), one
    )
    pbuf[4] = pbuf[3] * jnp.where(z >= 4, quad[0], one)

    in_copies[1].wait()
    lax.fori_loop(0, LOCAL_A, local_heads, 0)

    over_z(lambda o: p1_copy(o, o).wait_recv())
    cs = [decode(p1r.at[j]) for j in range(NZ)]
    b01, b45, b03, b07 = [], [], [], []
    for k in range(NSG):
        h = pl.ds(head_of(z, k), 1)
        d = [dtab[j, h, :] for j in range(NZ)]
        pr = [cs[2 * j][k] * d[2 * j + 1] + cs[2 * j + 1][k] for j in range(NZ // 2)]
        lo = pr[0] * (d[2] * d[3]) + pr[1]
        hi = pr[2] * (d[6] * d[7]) + pr[3]
        b01.append(pr[0])
        b45.append(pr[2])
        b03.append(lo)
        b07.append(lo * (d[4] * d[5] * d[6] * d[7]) + hi)
    osnd[3] = encode(b07)

    def x_copy(to, frm):
        return rcopy(osnd.at[3], tr.at[frm], x_s.at[to], x_r.at[frm], at(to, z, core))

    def x_to(o):
        return (o > x) & ((o < 3) | (x == 2))

    def send_x(o):
        @pl.when(x_to(o))
        def _():
            x_copy(o, x).start()

    over_x(send_x)
    osnd[2] = encode(b03)
    osnd[0] = encode(b01)
    osnd[1] = encode(b45)

    def sib_copy(lvl, o):
        dst = lbuf.at[lvl, core * NZ + o]
        return rcopy(dst, dst, sib_s.at[lvl, o], sib_r.at[lvl, o], sib)

    def sib_wait(lvl, o):
        dst = lbuf.at[lvl, (1 - core) * NZ + o]
        rcopy(dst, dst, sib_s.at[lvl, o], sib_r.at[lvl, o], sib).wait_recv()

    def bit(v, b):
        return lax.rem(v // 2**b, 2) == 1

    def keep(lvl, src):
        lbuf[lvl, me] = src
        sib_copy(lvl, z).start()

    def mir(o):
        return jnp.where(z >= 6, lax.rem(11 - o, NZ), o)

    l3_to = jnp.where(z >= 2, 4, 7)
    l3_end = (z == 4) | (z == 7)
    l3_mid = (z == 5) | (z == 6)

    def l3_own(do):
        @pl.when(z < 4)
        def _():
            do(lambda: l_copy(2, osnd.at[2], l3_to, z))

        @pl.when(z >= 4)
        def _():
            do(lambda: l_copy(2, osnd.at[2], jnp.where(l3_end, mir(5), mir(4)), z))
            do(lambda: l_copy(2, osnd.at[2], mir(6), z))

    def l3_on(slot, o, to):
        dst = lbuf.at[2, core * NZ + o]
        return rcopy(dst, dst, r3_s.at[slot, o], l_r.at[2, o], at(x, to, core))

    def l3_in(o):
        l_copy(2, lbuf.at[2, me], o, o).wait_recv()

    def l3_first():
        @pl.when(l3_end)
        def _():
            for q in (3, 2):
                o = mir(q)
                l3_in(o)
                l3_on(0, o, mir(5)).start()
                l3_on(1, o, mir(6)).start()
                sib_copy(2, o).start()

    def l3_middle():
        @pl.when(l3_mid)
        def _():
            for q in (6, 7, 0, 1):
                o = mir(q)
                l3_in(o)
                l3_on(0, o, mir(4)).start()
                sib_copy(2, o).start()

    def l3_rest():
        @pl.when(l3_mid)
        def _():
            for q in (4, 3, 2):
                o = mir(q)
                l3_in(o)
                sib_copy(2, o).start()

        @pl.when(l3_end)
        def _():
            for q in (5, 6, 7, 0, 1):
                o = mir(q)
                l3_in(o)
                sib_copy(2, o).start()

    def l3_on_done():
        @pl.when(l3_end)
        def _():
            for q in (3, 2):
                l3_on(0, mir(q), mir(5)).wait_send()
                l3_on(1, mir(q), mir(6)).wait_send()

        @pl.when(l3_mid)
        def _():
            for q in (6, 7, 0, 1):
                l3_on(0, mir(q), mir(4)).wait_send()

    def l2_own(do):
        for p in (2, 6):
            r = lax.rem(z + NZ - p, NZ)
            to = jnp.where((r == 1) | (r >= 5), p, p + 1)
            do(lambda to=to, p=p: l_copy(1, osnd.at[p // 4], to, z))

    l2_other = jnp.where(lax.rem(z, 2) == 0, z + 1, z - 1)

    def l2_off(d):
        return lax.rem(jnp.where(lax.rem(z, 2) == 0, z + NZ - d, z + d), NZ)

    def l2_on(o):
        dst = lbuf.at[1, core * NZ + o]
        return rcopy(dst, dst, r2_s.at[o], l_r.at[1, o], at(x, l2_other, core))

    def l2_in(o):
        l_copy(1, lbuf.at[1, me], o, o).wait_recv()

    def l2_first():
        @pl.when(bit(z, 1))
        def _():
            for d in (1, 2, 3):
                l2_in(l2_off(d))
                l2_on(l2_off(d)).start()
                sib_copy(1, l2_off(d)).start()

    def l2_rest():
        @pl.when(bit(z, 1))
        def _():
            for d in (7, 6, 5, 4):
                l2_in(l2_off(d))
                sib_copy(1, l2_off(d)).start()

    l3_own(lambda c: c().start())
    l2_own(lambda c: c().start())

    def l1_owner(do):
        for d in (1, 2, 3):
            to = zpeer(NZ - d)

            @pl.when(lax.rem(to, 2) == 1)
            def _(to=to):
                do(
                    lambda: l_copy(
                        0, p1r.at[lax.rem(to + NZ - 1, NZ)], to, z
                    )
                )

    @pl.when(lax.rem(z, 2) == 0)
    def _():
        l1_direct(lambda c: c.start())

    l1_owner(lambda c: c().start())

    @pl.when(lax.rem(z, 2) == 1)
    def _():
        keep(0, p1r[jnp.maximum(z - 1, 0)])

    @pl.when(z >= 4)
    def _():
        keep(2, osnd[2])

    @pl.when(bit(z, 1))
    def _():
        keep(1, osnd[z // 4])

    def sib_all(lvl):
        def go(o, _):
            sib_wait(lvl, o)
            return 0

        lax.fori_loop(0, NZ, go, 0)

    def far(level):
        def body(i, _):
            base = pl.multiple_of(i * PB, PB)
            if level == 0:
                state = sibe[pl.ds(base, PB), :].astype(BF16)
            else:
                parts = []
                for m in range(2):
                    v = decode(lbuf.at[level - 1, 2 * i + m])
                    for k in range(NSG):
                        p = pbuf[level, pl.ds(i * NSG + (m * NSG + k) // 2, 1), :]
                        parts.append((v[k] * p).astype(BF16))
                state = jnp.concatenate(parts, axis=0)
            read = lax.dot_general(
                state, quer[...], (((1,), (1,)), ((), ())), preferred_element_type=F32
            )
            for j in range(NSG):
                h = pl.ds(i * NSG + j, 1)
                coef = lam[9 + level, h, :] * entry[h, :]
                rows = pl.ds(pl.multiple_of(base + j * HD, HD), HD)
                acc[rows, :] = acc[rows, :] + read[j * HD : (j + 1) * HD] * coef
            return 0

        lax.fori_loop(0, NPB, body, 0)

    def gate_block(i, _):
        cols = pl.ds(pl.multiple_of(i * BR, BR), BR)
        v = gate[:, cols].astype(F32)
        gt[cols, :] = (v * (1.0 / (1.0 + jnp.exp(-v)))).T
        return 0

    lax.fori_loop(LOCAL_A, NB, local_heads, 0)
    in_copies[2].wait()
    lax.fori_loop(0, NB, gate_block, 0)

    def wait_e2(n, _):
        e_copy((1 - core) * (NPB // 2) + n).wait_recv()
        return 0

    lax.fori_loop(0, NPB // 2, wait_e2, 0)

    @pl.when(core == 1)
    def _():
        far(0)

    over_x(lambda o: dx_copy(o, o).wait_recv())
    pbuf[5] = pbuf[4] * jnp.where(lax.rem(x, 2) == 1, dline[jnp.maximum(x - 1, 0)], one)

    def x_in(frm):
        x_copy(frm, frm).wait_recv()

    NEAR = (6, 2, 7, 1)

    def spread(lvl, src):
        for d in NEAR:
            l_copy(lvl, src, zpeer(d), z).start()

    def r_copy(lvl, d, frm):
        dst = lbuf.at[lvl, core * NZ + frm]
        to = zpeer(d)
        return rcopy(dst, dst, r_s.at[to], l_r.at[lvl, frm], at(x, to, core))

    def up_copy(src, frm):
        return rcopy(
            src, lbuf.at[4, core * NZ + frm], up_s.at[frm], l_r.at[4, frm], at(xpeer(1), z, core)
        )

    def gather(lvl, up, first):
        def arrived(frm):
            l_copy(lvl, lbuf.at[lvl, me], frm, frm).wait_recv()

        def hand_on(frm):
            sib_copy(lvl, frm).start()
            if up:
                up_copy(lbuf.at[lvl, core * NZ + frm], frm).start()

        def pull(d):
            arrived(zpeer(d))
            hand_on(zpeer(d))

        if not first:
            for d in (1, 7, 3, 5, 4):
                pull(d)
            return
        arrived(zpeer(2))
        r_copy(lvl, 6, zpeer(2)).start()
        r_copy(lvl, 7, zpeer(2)).start()
        hand_on(zpeer(2))
        arrived(zpeer(6))
        r_copy(lvl, 1, zpeer(6)).start()
        hand_on(zpeer(6))

    def send_l4(frm):
        spread(3, tr.at[frm])
        keep(3, tr[frm])

    def send_l5():
        t0, t1 = decode(tr.at[0]), decode(tr.at[1])
        osnd[4] = encode(
            [t0[k] * dline[1, pl.ds(head_of(z, k), 1), :] + t1[k] for k in range(NSG)]
        )
        spread(4, osnd.at[4])
        up_copy(osnd.at[4], z).start()
        keep(4, osnd[4])

    @pl.when(x == 1)
    def _():
        x_in(0)
        send_l4(0)

    @pl.when(x == 3)
    def _():
        x_in(2)
        send_l4(2)

    @pl.when(x == 2)
    def _():
        x_in(1)
        x_in(0)
        send_l5()

    l3_first()
    l2_first()

    @pl.when(lax.rem(x, 2) == 1)
    def _():
        gather(3, False, True)

    @pl.when(x == 2)
    def _():
        gather(4, True, True)

    l3_middle()

    @pl.when(lax.rem(x, 2) == 1)
    def _():
        gather(3, False, False)

    @pl.when(x == 2)
    def _():
        gather(4, True, False)

    @pl.when(lax.rem(z, 2) == 1)
    def _():
        def go(o):
            l_copy(0, lbuf.at[0, me], o, o).wait_recv()
            sib_copy(0, o).start()

        over_z(go)

    l3_rest()
    l2_rest()

    @pl.when(lax.rem(z, 2) == 1)
    def _():
        sib_all(0)
        far(1)

    @pl.when(bit(z, 1))
    def _():
        sib_all(1)
        far(2)

    @pl.when(z >= 4)
    def _():
        sib_all(2)
        far(3)

    @pl.when(x == 3)
    def _():
        def go(o, _):
            up_copy(osnd.at[4], o).wait_recv()
            sib_copy(4, o).start()
            return 0

        lax.fori_loop(0, NZ, go, 0)

    @pl.when(lax.rem(x, 2) == 1)
    def _():
        sib_all(3)
        far(4)

    @pl.when(x >= 2)
    def _():
        sib_all(4)
        far(5)

    def gate_step(i, ssq):
        rows = pl.ds(pl.multiple_of(i * BR, BR), BR)
        v = acc[rows, :] * gt[rows, :]
        acc[rows, :] = v
        return ssq + jnp.sum((v * v).reshape(BR // 8, 8, TOK), axis=0)

    ssq = lax.fori_loop(0, NB, gate_step, jnp.zeros((8, TOK), F32))
    scale = lax.rsqrt(jnp.sum(ssq, axis=0, keepdims=True) * (1.0 / WIDTH) + EPS)

    def out_step(i, _):
        cols = pl.ds(pl.multiple_of(i * BR, BR), BR)
        v = (acc[cols, :] * scale).T
        out[:, cols] = (v * ng[cols].reshape(1, BR)).astype(BF16)
        return 0

    lax.fori_loop(0, NB, out_step, 0)

    halo_copy.wait_send()
    th_copy.wait_send()

    def e_done(i, _):
        e_copy(i).wait_send()
        return 0

    lax.fori_loop(0, NPB, e_done, 0)
    over_z(lambda o: dz_copy(o, z).wait_send())
    over_z(lambda o: p1_copy(o, z).wait_send())
    over_x(lambda o: dx_copy(o, x).wait_send())

    def x_done(o):
        @pl.when(x_to(o))
        def _():
            x_copy(o, x).wait_send()

    over_x(x_done)

    l3_own(lambda c: c().wait_send())
    l3_on_done()
    l2_own(lambda c: c().wait_send())

    @pl.when(bit(z, 1))
    def _():
        for d in (1, 2, 3):
            l2_on(l2_off(d)).wait_send()

    def spread_done(lvl):
        for d in NEAR:
            l_copy(lvl, osnd.at[4], zpeer(d), z).wait_send()
        for d in (1, 7, 6):
            r_copy(lvl, d, z).wait_send()

    pl.when(lax.rem(x, 2) == 1)(lambda: spread_done(3))

    @pl.when(x == 2)
    def _():
        spread_done(4)

        def go(o, _):
            up_copy(osnd.at[4], o).wait_send()
            return 0

        lax.fori_loop(0, NZ, go, 0)

    def sib_done(lvl):
        def go(o, _):
            sib_copy(lvl, o).wait_send()
            return 0

        lax.fori_loop(0, NZ, go, 0)

    @pl.when(lax.rem(z, 2) == 0)
    def _():
        l1_direct(lambda c: c.wait_send())

    l1_owner(lambda c: c().wait_send())
    pl.when(lax.rem(z, 2) == 1)(lambda: sib_done(0))
    pl.when(bit(z, 1))(lambda: sib_done(1))
    pl.when(z >= 4)(lambda: sib_done(2))
    pl.when(lax.rem(x, 2) == 1)(lambda: sib_done(3))
    pl.when(x >= 2)(lambda: sib_done(4))


def per_device(
    mixed_input,
    conv_weight,
    conv_bias,
    gate_input,
    log_decay,
    level_weights,
    skip_gain,
    norm_gain,
    seg_lengths,
):
    vmem = pl.BlockSpec(memory_space=pltpu.VMEM)
    hbm = pl.BlockSpec(memory_space=pl.ANY)
    smem = pl.BlockSpec(memory_space=pltpu.SMEM)
    dma = pltpu.SemaphoreType.DMA
    return pl.pallas_call(
        kernel,
        out_shape=pltpu.VMEM((TOK, WIDTH), BF16),
        in_specs=[hbm, hbm, vmem, hbm] + [vmem] * 3 + [smem] * 2,
        out_specs=vmem,
        scratch_shapes=[
            pltpu.VMEM((TOK, CH), BF16),
            pltpu.VMEM((TOK, WIDTH), BF16),
            pltpu.VMEM((20, HEADS, TOK), F32),
            pltpu.VMEM((HALO, CH), BF16),
            pltpu.VMEM((TOK + 8, BR), F32),
            pltpu.VMEM((TOK, CH), F32),
            pltpu.VMEM((WIDTH, TOK), BF16),
            pltpu.VMEM((TOK, STATE), BF16),
            pltpu.VMEM((TOK, STATE), BF16),
            pltpu.VMEM((WIDTH, STATE), F32),
            pltpu.VMEM((WIDTH, STATE), F32),
            pltpu.VMEM((NZ, XP, STATE), jnp.int16),
            pltpu.VMEM((NZ, XP, STATE), jnp.int16),
            pltpu.VMEM((5, XP, STATE), jnp.int16),
            pltpu.VMEM((NX, XP, STATE), jnp.int16),
            pltpu.VMEM((5, 2 * NZ, XP, STATE), jnp.int16),
            pltpu.VMEM((NZ, HEADS, 128), F32),
            pltpu.VMEM((NX, HEADS, 128), F32),
            pltpu.VMEM((2, HEADS, 128), F32),
            pltpu.VMEM((6, HEADS, 128), F32),
            pltpu.VMEM((HEADS, TOK), F32),
            pltpu.VMEM((TOK, 128), F32),
            pltpu.VMEM((HEADS, TOK), F32),
            pltpu.VMEM((HEADS, TOK), F32),
            pltpu.VMEM((TOK, TOK), F32),
            pltpu.VMEM((128, 128), jnp.int32),
            pltpu.VMEM((WIDTH, TOK), F32),
            pltpu.VMEM((WIDTH, TOK), F32),
            dma((3,)),
            dma,
            dma,
            dma,
            dma,
            dma((NPB,)),
            dma((NPB,)),
            dma((NZ,)),
            dma((NZ,)),
            dma((NX,)),
            dma((NX,)),
            dma((NZ,)),
            dma((NZ,)),
            dma((5, NZ)),
            dma((5, NZ)),
            dma((NZ,)),
            dma((NZ,)),
            dma((2, NZ)),
            dma((NZ,)),
            dma((NZ,)),
            dma((NX,)),
            dma((NX,)),
            dma((5, NZ)),
            dma((5, NZ)),
        ],
        compiler_params=pltpu.CompilerParams(
            collective_id=0, has_side_effects=True, vmem_limit_bytes=60 * 1024 * 1024
        ),
        name="layer",
    )(
        mixed_input,
        gate_input,
        log_decay,
        jnp.transpose(level_weights, (1, 0, 2)),
        conv_weight,
        conv_bias,
        norm_gain,
        skip_gain,
        seg_lengths,
    )


def solution(mesh):
    in_specs = (
        P(("batch", "group"), None),
        P(),
        P(),
        P(("batch", "group"), None),
        P(None, ("batch", "group")),
        P(None, None, ("batch", "group")),
        P(),
        P(),
        P("batch"),
    )
    out_specs = P(("batch", "group"), None)
    return jax.shard_map(
        per_device, mesh=mesh, in_specs=in_specs, out_specs=out_specs, check_vma=False
    )
```
